32 devices in a mesh: seq: 8 (over z, x), head: 4 (over y, core).
Axes of the slice: x: 2, y: 2, z: 4, core: 2. Of those that a mesh axis runs over, the one named last changes fastest.
Arguments:
- queries: bfloat16 [8192, 4096], P('seq', 'head'), may hold values from -6 to 6
- keys: bfloat16 [8192, 4096], P('seq', 'head'), may hold values from -6 to 6
- values: bfloat16 [8192, 4096], P('seq', 'head'), may hold values from -120 to 120
- gain: float32 [4096], P('head'), may hold values from 0.1 to 1.9
- out_grad: bfloat16 [8192, 4096], P('seq', 'head'), may hold values from -6 to 6
Outputs:
- mixed: bfloat16 [8192, 4096], P('seq', 'head')
- query_grad: bfloat16 [8192, 4096], P('seq', 'head')
- key_grad: bfloat16 [8192, 4096], P('seq', 'head')
- value_grad: bfloat16 [8192, 4096], P('seq', 'head')
The draws below stay inside these ranges and needn't reach their ends.
All inputs are finite; a program needn't handle non-finite values.
Results may differ from the reference program's by a relative error of at most 0.0058.
Values sent between devices are 32-bit elements; how exact they have to be, the bound alone decides.
No kernel may reach another device: no remote copies, remote signals or barrier semaphores. Data moves between devices by JAX's collectives and lax.ppermute only.
A program may use at most 128 MiB of HBM per device.

```python
import math
import jax
import jax.numpy as jnp
from jax import lax

HEADS = 32
HEAD_DIM = 128
BLOCK = 128
TOKENS = 8192
WIDTH = 4096


def draw_values(key, part):
    noise_key, head_key, row_key = jax.random.split(key, 3)
    head_scale = jnp.exp(jax.random.uniform(head_key, (WIDTH // HEAD_DIM,), jnp.float32, 0.0, math.log(10.0)))
    column_scale = jnp.repeat(head_scale, HEAD_DIM)[None, :]
    row_scale = jnp.exp(jax.random.uniform(row_key, (TOKENS, 1), jnp.float32, 0.0, math.log(10.0)))
    noise_draw = jax.random.normal(noise_key, (TOKENS, WIDTH), jnp.float32)
    noise_draw = jnp.clip(noise_draw, -4.0, 4.0)
    return (0.3 * noise_draw * row_scale * column_scale).astype(jnp.bfloat16)


def shard_levels(stream_key, extent, shards, smallest, high):
    loudness, own = 1.0, jax.random.fold_in(stream_key, 6)
    for position, blocks in shards:
        heights = jnp.exp(jax.random.uniform(jax.random.fold_in(own, position), (blocks,), jnp.float32, smallest / len(shards), high / len(shards)))
        loudness = loudness * jnp.repeat(heights, extent[position] // blocks).reshape([-1 if axis == position else 1 for axis in range(len(extent))])
    return loudness


def noise(rng, extent, width, bound, shards=(), held_as=jnp.bfloat16):
    drawn = jax.random.normal(rng, extent, jnp.float32) * width
    if len(shards) > 0:
        drawn = shard_levels(rng, extent, shards, -0.22, 0.18) * drawn
    return jnp.clip(drawn, min=-bound, max=bound).astype(held_as)


def setup_inputs(seed: int = 0) -> dict:
    streams_of = jax.random.split(jax.random.key(seed), 6)
    queries = noise(streams_of[0], (TOKENS, WIDTH), 1.0, 6.0, ((0, 8), (1, 4)))
    keys = noise(streams_of[1], (TOKENS, WIDTH), 1.0, 6.0, ((0, 8), (1, 4)))
    values = draw_values(jax.random.fold_in(streams_of[5], 71), 0)
    gain = jnp.clip(1.0 + 0.18 * jax.random.normal(streams_of[3], (WIDTH,), jnp.float32), 0.1, 1.9)
    out_grad = noise(streams_of[4], (TOKENS, WIDTH), 1.0, 6.0, ((0, 8), (1, 4)))
    return dict(queries=queries, keys=keys, values=values, gain=gain, out_grad=out_grad)


epsilon = 1e-05
highest = lax.Precision.HIGHEST

def rounded(array_in):
    return lax.optimization_barrier(array_in.astype(jnp.bfloat16)).astype(jnp.float32)

def to_blocks(array_in):
    block_count = TOKENS // BLOCK
    return array_in.reshape(block_count, BLOCK, HEADS, HEAD_DIM).transpose(0, 2, 1, 3)

def from_blocks(array_in):
    return array_in.transpose(0, 2, 1, 3).reshape(TOKENS, WIDTH)

def reference(queries, keys, values, gain, out_grad):
    causal = jnp.tril(jnp.ones((BLOCK, BLOCK), dtype=bool))
    query_blocks = to_blocks(queries)
    key_blocks = to_blocks(keys)
    value_blocks = to_blocks(values)

    def forward(prefix, inputs):
        query_rows = inputs[0].astype(jnp.float32)
        key_rows = inputs[1].astype(jnp.float32)
        value_rows = inputs[2].astype(jnp.float32)
        scores = jnp.einsum('hid,hjd->hij', query_rows, key_rows, precision=highest)
        weights = rounded(jnp.where(causal, scores, 0.0))
        prefix_low = rounded(prefix)
        within = jnp.einsum('hij,hjd->hid', weights, value_rows, precision=highest)
        across = jnp.einsum('hid,hde->hie', query_rows, prefix_low, precision=highest)
        block_state = jnp.einsum('hjd,hje->hde', key_rows, value_rows, precision=highest)
        return (prefix + block_state, (within + across, prefix_low))
    start_state = jnp.zeros((HEADS, HEAD_DIM, HEAD_DIM), jnp.float32)
    last_state, (attended_blocks, prefix_lows) = lax.scan(forward, start_state, (query_blocks, key_blocks, value_blocks))
    attended = from_blocks(attended_blocks)
    squares = lax.optimization_barrier(jnp.sum(attended * attended, axis=1))
    inverse = lax.rsqrt(squares / WIDTH + epsilon)
    mixed = (gain[None, :] * attended * inverse[:, None]).astype(jnp.bfloat16)
    scaled = gain[None, :] * out_grad.astype(jnp.float32)
    dots = lax.optimization_barrier(jnp.sum(scaled * attended, axis=1))
    grad_attn = (inverse[:, None] * scaled - (inverse ** 3 * dots / WIDTH)[:, None] * attended).astype(jnp.bfloat16)
    grad_blocks = to_blocks(grad_attn)

    def backward(suffix, inputs):
        query_rows = inputs[0].astype(jnp.float32)
        key_rows = inputs[1].astype(jnp.float32)
        value_rows = inputs[2].astype(jnp.float32)
        grad_rows = inputs[3].astype(jnp.float32)
        prefix_low = inputs[4]
        scores = jnp.einsum('hid,hjd->hij', query_rows, key_rows, precision=highest)
        weights = rounded(jnp.where(causal, scores, 0.0))
        back_scores = jnp.einsum('hie,hje->hij', grad_rows, value_rows, precision=highest)
        back_weights = rounded(jnp.where(causal, back_scores, 0.0))
        suffix_low = rounded(suffix)
        query_part = jnp.einsum('hij,hjd->hid', back_weights, key_rows, precision=highest) + jnp.einsum('hie,hde->hid', grad_rows, prefix_low, precision=highest)
        key_part = jnp.einsum('hij,hid->hjd', back_weights, query_rows, precision=highest) + jnp.einsum('hje,hde->hjd', value_rows, suffix_low, precision=highest)
        value_part = jnp.einsum('hij,hie->hje', weights, grad_rows, precision=highest) + jnp.einsum('hjd,hde->hje', key_rows, suffix_low, precision=highest)
        block_state = jnp.einsum('hid,hie->hde', query_rows, grad_rows, precision=highest)
        return (suffix + block_state, (query_part, key_part, value_part))
    end_state, (query_parts, key_parts, value_parts) = lax.scan(backward, start_state, (query_blocks, key_blocks, value_blocks, grad_blocks, prefix_lows), reverse=True)
    query_grad = from_blocks(query_parts).astype(jnp.bfloat16)
    key_grad = from_blocks(key_parts).astype(jnp.bfloat16)
    value_grad = from_blocks(value_parts).astype(jnp.bfloat16)
    return (mixed, query_grad, key_grad, value_grad)
```

```python
import functools

import jax
import jax.numpy as jnp
from jax import lax
from jax.experimental import pallas as pl
from jax.experimental.pallas import tpu as pltpu
from jax.sharding import PartitionSpec as P

HEAD_DIM = 128
BLOCK = 128
WIDTH = 4096
epsilon = 1e-05

F32 = jnp.float32
BF16 = jnp.bfloat16


def dot(a, b, ca, cb):
    return lax.dot_general(a, b, (((ca,), (cb,)), ((), ())), preferred_element_type=F32)


def causal_mask():
    row = lax.broadcasted_iota(jnp.int32, (BLOCK, BLOCK), 0)
    col = lax.broadcasted_iota(jnp.int32, (BLOCK, BLOCK), 1)
    return col <= row


def rows_of(n):
    return pl.ds(n * BLOCK, BLOCK)


def state_kernel(k_ref, v_ref, t_ref):
    t_ref[0] = dot(k_ref[...], v_ref[...], 0, 0)


def local_kernel(blocks, q_ref, k_ref, v_ref, w_ref, a_ref):
    causal = causal_mask()
    prefix = jnp.zeros((HEAD_DIM, HEAD_DIM), F32)
    for n in range(blocks):
        q, k, v = q_ref[rows_of(n), :], k_ref[rows_of(n), :], v_ref[rows_of(n), :]
        w = jnp.where(causal, dot(q, k, 1, 1), 0.0).astype(BF16)
        w_ref[rows_of(n), :] = w
        out = dot(w, v, 1, 0)
        if n > 0:
            out = out + dot(q, prefix.astype(BF16), 1, 0)
        a_ref[rows_of(n), :] = out
        if n + 1 < blocks:
            prefix = prefix + dot(k, v, 0, 0)


def stats_kernel(a_in, q_ref, p_ref, og_ref, gain_ref, a_ref, s_ref, sq, dt):
    h = pl.program_id(0)
    att = a_in[...] + dot(q_ref[...], p_ref[0].astype(BF16), 1, 0)
    a_ref[...] = att
    scaled = gain_ref[...] * og_ref[...].astype(F32)

    @pl.when(h == 0)
    def _():
        sq[...] = att * att
        dt[...] = scaled * att

    @pl.when(h > 0)
    def _():
        sq[...] += att * att
        dt[...] += scaled * att

    @pl.when(h == pl.num_programs(0) - 1)
    def _():
        for n in range(att.shape[0] // BLOCK):
            cols = pl.ds(n * BLOCK, BLOCK)
            s_ref[0:1, cols] = jnp.sum(sq[rows_of(n), :].T, axis=0, keepdims=True)
            s_ref[1:2, cols] = jnp.sum(dt[rows_of(n), :].T, axis=0, keepdims=True)


def norm_kernel(a_ref, q_ref, og_ref, gain_ref, s_ref, m_ref, g_ref, t_ref, inv, coef):
    h = pl.program_id(0)

    @pl.when(h == 0)
    def _():
        inverse = lax.rsqrt(s_ref[0:1, :] / WIDTH + epsilon)
        factor = inverse * inverse * inverse * s_ref[1:2, :] / WIDTH
        for n in range(a_ref.shape[0] // BLOCK):
            lo, hi = n * BLOCK, (n + 1) * BLOCK
            inv[rows_of(n), :] = jnp.broadcast_to(inverse[:, lo:hi], (BLOCK, BLOCK)).T
            coef[rows_of(n), :] = jnp.broadcast_to(factor[:, lo:hi], (BLOCK, BLOCK)).T

    att = a_ref[...]
    gain = gain_ref[...]
    m_ref[...] = (gain * att * inv[...]).astype(BF16)
    grad = (inv[...] * (gain * og_ref[...].astype(F32)) - coef[...] * att).astype(BF16)
    g_ref[...] = grad
    t_ref[0] = dot(q_ref[...], grad, 0, 0)


def back_kernel(blocks, q_ref, k_ref, v_ref, w_ref, g_ref, p_ref, qg_ref, kl_ref, vl_ref, bw):
    causal = causal_mask()
    prefix = p_ref[0]
    for n in range(blocks):
        k, v, g = k_ref[rows_of(n), :], v_ref[rows_of(n), :], g_ref[rows_of(n), :]
        b = jnp.where(causal, dot(g, v, 1, 1), 0.0).astype(BF16)
        bw[rows_of(n), :] = b
        qg_ref[rows_of(n), :] = (dot(b, k, 1, 0) + dot(g, prefix.astype(BF16), 1, 1)).astype(BF16)
        if n + 1 < blocks:
            prefix = prefix + dot(k, v, 0, 0)
    suffix = jnp.zeros((HEAD_DIM, HEAD_DIM), F32)
    for n in reversed(range(blocks)):
        q, k, v = q_ref[rows_of(n), :], k_ref[rows_of(n), :], v_ref[rows_of(n), :]
        g = g_ref[rows_of(n), :]
        kp = dot(bw[rows_of(n), :], q, 0, 0)
        vp = dot(w_ref[rows_of(n), :], g, 0, 0)
        if n + 1 < blocks:
            low = suffix.astype(BF16)
            kp = kp + dot(v, low, 1, 1)
            vp = vp + dot(k, low, 1, 0)
        kl_ref[rows_of(n), :] = kp
        vl_ref[rows_of(n), :] = vp
        if n > 0:
            suffix = suffix + dot(q, g, 0, 0)


def last_kernel(k_ref, v_ref, kl_ref, vl_ref, s_ref, kg_ref, vg_ref):
    low = s_ref[0].astype(BF16)
    kg_ref[...] = (kl_ref[...] + dot(v_ref[...], low, 1, 1)).astype(BF16)
    vg_ref[...] = (vl_ref[...] + dot(k_ref[...], low, 1, 0)).astype(BF16)


def call(kernel, heads, rows, ins, outs, scratch=(), flops=0, nbytes=0, vmem=16):
    specs = {
        "tok": pl.BlockSpec((rows, HEAD_DIM), lambda h: (0, h)),
        "state": pl.BlockSpec((1, HEAD_DIM, HEAD_DIM), lambda h: (h, 0, 0)),
        "gain": pl.BlockSpec((1, HEAD_DIM), lambda h: (0, h)),
        "row": pl.BlockSpec((2, rows), lambda h: (0, 0)),
    }
    shapes = {
        "tok": (rows, heads * HEAD_DIM),
        "state": (heads, HEAD_DIM, HEAD_DIM),
        "row": (2, rows),
    }
    return pl.pallas_call(
        kernel,
        grid=(heads,),
        in_specs=[specs[kind] for kind, _ in ins],
        out_specs=tuple(specs[kind] for kind, _ in outs),
        out_shape=tuple(jax.ShapeDtypeStruct(shapes[kind], dtype) for kind, dtype in outs),
        scratch_shapes=list(scratch),
        compiler_params=pltpu.CompilerParams(vmem_limit_bytes=vmem << 20),
        cost_estimate=pl.CostEstimate(flops=flops, bytes_accessed=nbytes, transcendentals=0),
    )(*[a for _, a in ins])


def seq_scan(states, size, own, reverse):
    place = (lambda i: size - 1 - i) if reverse else (lambda i: i)
    send = lambda a, pairs: lax.ppermute(a, "seq", [(place(i), place(j)) for i, j in pairs])
    if size % 2:
        raise ValueError("odd seq")
    outer = size // 2
    swap = [(i, i ^ 1) for i in range(size)]
    parity = own % 2
    low = parity == 0
    first = (parity == 1) if reverse else low
    outs = []
    for t in states:
        half = t.shape[0] // 2
        mine = jnp.where(low, t[:half], t[half:])
        other = jnp.where(low, t[half:], t[:half])
        got = send(other, swap)
        pair = mine + got
        if outer <= 4:
            running, total = pair, jnp.zeros_like(pair)
            for hop in range(outer - 1):
                r = send(running, [(2 * hop, 2 * hop + 2), (2 * hop + 1, 2 * hop + 3)])
                total = total + r
                running = r + pair
        else:
            total = send(pair, [(i, i + 2) for i in range(size - 2)])
            step = 1
            while step < outer - 1:
                total = total + send(total, [(i, i + 2 * step) for i in range(size - 2 * step)])
                step *= 2
        answer = send(jnp.where(first, total + mine, total), swap)
        kept = jnp.where(first, total, total + got)
        outs.append(jnp.concatenate([jnp.where(low, kept, answer), jnp.where(low, answer, kept)], axis=0))
    return outs


def head_sum(a, size):
    step = 1
    while step < size:
        a = a + lax.ppermute(a, "head", [(i, i ^ step) for i in range(size)])
        step *= 2
    return a


def body(seq_size, head_size, queries, keys, values, gain, out_grad):
    rows, width = queries.shape
    blocks, heads = rows // BLOCK, width // HEAD_DIM
    own = lax.axis_index("seq")
    gain = gain.reshape(1, width)
    run = functools.partial(call, heads=heads, rows=rows)
    unit = 2 * rows * HEAD_DIM * HEAD_DIM * heads
    tok = rows * width
    chunk = max(2, 2 * (heads // 8))

    def split(t):
        return [t[i : i + chunk] for i in range(0, heads, chunk)]

    (state,) = run(state_kernel, ins=[("tok", keys), ("tok", values)], outs=[("state", F32)], flops=unit, nbytes=4 * tok)
    weights, local = run(
        functools.partial(local_kernel, blocks),
        ins=[("tok", queries), ("tok", keys), ("tok", values)],
        outs=[("tok", BF16), ("tok", F32)],
        flops=4 * unit,
        nbytes=12 * tok,
    )
    prefix = jnp.concatenate(seq_scan(split(state), seq_size, own, False), axis=0)
    attended, sums = run(
        stats_kernel,
        ins=[("tok", local), ("tok", queries), ("state", prefix), ("tok", out_grad), ("gain", gain)],
        outs=[("tok", F32), ("row", F32)],
        scratch=[pltpu.VMEM((rows, HEAD_DIM), F32)] * 2,
        flops=unit,
        nbytes=12 * tok,
    )
    sums = head_sum(sums, head_size)
    mixed, grad, back = run(
        norm_kernel,
        ins=[("tok", attended), ("tok", queries), ("tok", out_grad), ("gain", gain), ("row", sums)],
        outs=[("tok", BF16), ("tok", BF16), ("state", F32)],
        scratch=[pltpu.VMEM((rows, HEAD_DIM), F32)] * 2,
        flops=unit,
        nbytes=12 * tok,
    )
    query_grad, key_local, value_local = run(
        functools.partial(back_kernel, blocks),
        ins=[("tok", queries), ("tok", keys), ("tok", values), ("tok", weights), ("tok", grad), ("state", prefix)],
        outs=[("tok", BF16), ("tok", F32), ("tok", F32)],
        scratch=[pltpu.VMEM((rows, BLOCK), BF16)],
        flops=9 * unit,
        nbytes=20 * tok,
    )
    suffix = jnp.concatenate(seq_scan(split(back), seq_size, own, True), axis=0)
    key_grad, value_grad = run(
        last_kernel,
        ins=[("tok", keys), ("tok", values), ("tok", key_local), ("tok", value_local), ("state", suffix)],
        outs=[("tok", BF16), ("tok", BF16)],
        flops=2 * unit,
        nbytes=16 * tok,
    )
    return mixed, query_grad, key_grad, value_grad


def solution(mesh):
    placed = (P("seq", "head"), P("seq", "head"), P("seq", "head"), P("head"), P("seq", "head"))
    return jax.shard_map(
        functools.partial(body, mesh.shape["seq"], mesh.shape["head"]),
        mesh=mesh,
        in_specs=placed,
        out_specs=(P("seq", "head"),) * 4,
        check_vma=False,
    )
```

```python
import functools

import jax
import jax.numpy as jnp
from jax import lax
from jax.experimental import pallas as pl
from jax.experimental.pallas import tpu as pltpu
from jax.sharding import PartitionSpec as P

HEAD_DIM = 128
BLOCK = 128
WIDTH = 4096
epsilon = 1e-05

F32 = jnp.float32
BF16 = jnp.bfloat16
VMEM = pl.BlockSpec(memory_space=pltpu.VMEM)
HBM = pl.BlockSpec(memory_space=pltpu.HBM)


def dot(a, b, ca, cb):
    return lax.dot_general(a, b, (((ca,), (cb,)), ((), ())), preferred_element_type=F32)


def causal_mask():
    row = lax.broadcasted_iota(jnp.int32, (BLOCK, BLOCK), 0)
    col = lax.broadcasted_iota(jnp.int32, (BLOCK, BLOCK), 1)
    return col <= row


def rows_of(n):
    return slice(n * BLOCK, (n + 1) * BLOCK)


def cols_of(h):
    return slice(h * HEAD_DIM, (h + 1) * HEAD_DIM)


def cols_at(h):
    return pl.ds(pl.multiple_of(h * HEAD_DIM, HEAD_DIM), HEAD_DIM)


def state_kernel(first, heads, k_hbm, v_hbm, k_ref, v_ref, t_ref, sems):
    copies = []
    for h in range(heads):
        for i, (src, dst) in enumerate(((k_hbm, k_ref), (v_hbm, v_ref))):
            copies.append(pltpu.make_async_copy(src.at[:, cols_of(first + h)], dst.at[:, cols_of(h)], sems.at[i, h]))
            copies[-1].start()
    for h in range(heads):
        copies[2 * h].wait()
        copies[2 * h + 1].wait()
        t_ref[h] = dot(k_ref[:, cols_of(h)], v_ref[:, cols_of(h)], 0, 0)


def local_kernel(first, heads, blocks, q_ref, k_ref, v_ref, w_ref, a_ref, low):
    causal = causal_mask()

    def head(h, carry):
        c, cq = cols_at(h), cols_at(h + first)
        for n in range(0, blocks, 2):
            if n + 1 < blocks:
                both = slice(n * BLOCK, (n + 2) * BLOCK)
                s = dot(q_ref[both, cq], k_ref[both, c], 1, 1)
                w_ref[rows_of(n), c] = jnp.where(causal, s[:BLOCK, :BLOCK], 0.0).astype(BF16)
                w_ref[rows_of(n + 1), c] = jnp.where(causal, s[BLOCK:, BLOCK:], 0.0).astype(BF16)
            else:
                s = dot(q_ref[rows_of(n), cq], k_ref[rows_of(n), c], 1, 1)
                w_ref[rows_of(n), c] = jnp.where(causal, s, 0.0).astype(BF16)
        prefix = None
        for n in range(blocks - 1):
            s = dot(k_ref[rows_of(n), c], v_ref[rows_of(n), c], 0, 0)
            prefix = s if prefix is None else prefix + s
            low[rows_of(n), :] = prefix.astype(BF16)
        a_ref[rows_of(0), c] = dot(w_ref[rows_of(0), c], v_ref[rows_of(0), c], 1, 0)
        for n in range(1, blocks):
            left = jnp.concatenate([w_ref[rows_of(n), c], q_ref[rows_of(n), cq]], axis=1)
            right = jnp.concatenate([v_ref[rows_of(n), c], low[rows_of(n - 1), :]], axis=0)
            a_ref[rows_of(n), c] = dot(left, right, 1, 0)
        return carry

    lax.fori_loop(0, heads, head, 0, unroll=2)


def stats_kernel(first, heads, blocks, a_in, q_ref, p_ref, og_ref, gain_ref, a_ref, s_ref):
    low = [p_ref[h].astype(BF16) for h in range(heads)]
    for n in range(blocks):
        r = rows_of(n)
        squares = dots = None
        for h in range(heads):
            c, cq = cols_of(h), cols_of(first + h)
            att = a_in[r, c] + dot(q_ref[r, cq], low[h], 1, 0)
            a_ref[r, c] = att
            scaled = gain_ref[:, cq] * og_ref[r, cq].astype(F32)
            squares = att * att if squares is None else squares + att * att
            dots = scaled * att if dots is None else dots + scaled * att
        s_ref[0:1, r] = jnp.sum(squares.T, axis=0, keepdims=True)
        s_ref[1:2, r] = jnp.sum(dots.T, axis=0, keepdims=True)


def factor_kernel(blocks, s_ref, inv_ref, coef_ref):
    inverse = lax.rsqrt(s_ref[0:1, :] / WIDTH + epsilon)
    factor = inverse * inverse * inverse * s_ref[1:2, :] / WIDTH
    for n in range(blocks):
        inv_ref[rows_of(n), :] = jnp.broadcast_to(inverse[:, rows_of(n)], (BLOCK, BLOCK)).T
        coef_ref[rows_of(n), :] = jnp.broadcast_to(factor[:, rows_of(n)], (BLOCK, BLOCK)).T


def grad_kernel(first, heads, a_ref, q_ref, og_ref, gain_ref, inv_ref, coef_ref, g_ref, t_ref):
    for h in range(heads):
        c, cq = cols_of(h), cols_of(first + h)
        scaled = gain_ref[:, cq] * og_ref[:, cq].astype(F32)
        grad = (inv_ref[...] * scaled - coef_ref[...] * a_ref[:, c]).astype(BF16)
        g_ref[:, c] = grad
        t_ref[h] = dot(q_ref[:, cq], grad, 0, 0)


def mixed_kernel(parts, heads, *refs):
    a_refs, (gain_ref, inv_ref, m_ref) = refs[:parts], refs[parts:]
    for p, a_ref in enumerate(a_refs):
        for h in range(heads):
            cq = cols_of(p * heads + h)
            m_ref[:, cq] = (gain_ref[:, cq] * a_ref[:, cols_of(h)] * inv_ref[...]).astype(BF16)


def back_kernel(first, inner, heads, blocks, q_ref, k_ref, v_ref, w_ref, g_ref, p_ref, *rest):
    qg_hbm, kl_ref, vl_ref, qg, bw, plow, slow, sems = rest[-8:]
    causal = causal_mask()

    def copy_out(h, c, cq):
        return pltpu.make_async_copy(qg.at[:, c], qg_hbm.at[:, cq], sems.at[h])

    def head(h, carry):
        c, ci, cq = cols_at(h), cols_at(h + inner), cols_at(h + first)
        for n in range(blocks):
            r = rows_of(n)
            bw[r, :] = jnp.where(causal, dot(g_ref[r, ci], v_ref[r, ci], 1, 1), 0.0).astype(BF16)
        prefix = p_ref[h + inner]
        plow[rows_of(0), :] = prefix.astype(BF16)
        for n in range(blocks - 1):
            prefix = prefix + dot(k_ref[rows_of(n), ci], v_ref[rows_of(n), ci], 0, 0)
            plow[rows_of(n + 1), :] = prefix.astype(BF16)
        suffix = None
        for n in reversed(range(1, blocks)):
            s = dot(q_ref[rows_of(n), cq], g_ref[rows_of(n), ci], 0, 0)
            suffix = s if suffix is None else suffix + s
            slow[rows_of(n - 1), :] = suffix.astype(BF16)
        for n in range(blocks):
            r = rows_of(n)
            q, k, v, g = q_ref[r, cq], k_ref[r, ci], v_ref[r, ci], g_ref[r, ci]
            qg[r, c] = (dot(bw[r, :], k, 1, 0) + dot(g, plow[r, :], 1, 1)).astype(BF16)
            kp, vp = dot(bw[r, :], q, 0, 0), dot(w_ref[r, ci], g, 0, 0)
            if n + 1 < blocks:
                kp, vp = kp + dot(v, slow[r, :], 1, 1), vp + dot(k, slow[r, :], 1, 0)
            kl_ref[r, c] = kp
            vl_ref[r, c] = vp
        copy_out(h, c, cq).start()
        return carry

    lax.fori_loop(0, heads, head, 0, unroll=2)
    for h in range(heads):
        copy_out(h, cols_of(h), cols_of(h + first)).wait()


def last_kernel(first, pieces, heads, k_ref, v_ref, s_ref, *rest):
    kls, vls = rest[:pieces], rest[pieces : 2 * pieces]
    kg_hbm, vg_hbm, kg, vg, sems = rest[-5:]
    copies = []
    for p in range(pieces):
        for i in range(heads):
            h = p * heads + i
            c, cq = cols_of(h), cols_of(first + h)
            low = s_ref[h].astype(BF16)
            kg[:, c] = (kls[p][:, cols_of(i)] + dot(v_ref[:, c], low, 1, 1)).astype(BF16)
            copies.append(pltpu.make_async_copy(kg.at[:, c], kg_hbm.at[:, cq], sems.at[0, h]))
            copies[-1].start()
            vg[:, c] = (vls[p][:, cols_of(i)] + dot(k_ref[:, c], low, 1, 0)).astype(BF16)
            copies.append(pltpu.make_async_copy(vg.at[:, c], vg_hbm.at[:, cq], sems.at[1, h]))
            copies[-1].start()
    for copy in copies:
        copy.wait()


def call(kernel, ins, outs, in_specs=None, out_specs=None, scratch=(), aliases=None, flops=0, vmem=6):
    nbytes = sum(a.size * a.dtype.itemsize for a in ins)
    return pl.pallas_call(
        kernel,
        in_specs=in_specs or [VMEM] * len(ins),
        out_specs=tuple(out_specs or [VMEM] * len(outs)),
        out_shape=tuple(jax.ShapeDtypeStruct(shape, dtype) for shape, dtype in outs),
        scratch_shapes=list(scratch),
        input_output_aliases=aliases or {},
        compiler_params=pltpu.CompilerParams(vmem_limit_bytes=vmem << 20),
        cost_estimate=pl.CostEstimate(flops=flops, bytes_accessed=nbytes, transcendentals=0),
    )(*ins)


def scan_stages(states, size, own, reverse):
    place = (lambda i: size - 1 - i) if reverse else (lambda i: i)
    perm = lambda pairs: [(place(i), place(j)) for i, j in pairs]
    outer = size // 2
    swap = [(i, i ^ 1) for i in range(size)]
    low = own % 2 == 0
    first = own % 2 == (1 if reverse else 0)
    half = states.shape[0] // 2
    mine = jnp.where(low, states[:half], states[half:])
    other = jnp.where(low, states[half:], states[:half])
    got = yield other, perm(swap)
    pair = mine + got
    total = None
    if outer <= 4:
        running = pair
        for hop in range(outer - 1):
            r = yield running, perm([(2 * hop, 2 * hop + 2), (2 * hop + 1, 2 * hop + 3)])
            total = r if total is None else total + r
            running = r + pair
    else:
        total = yield pair, perm([(i, i + 2) for i in range(size - 2)])
        step = 1
        while step < outer - 1:
            r = yield total, perm([(i, i + 2 * step) for i in range(size - 2 * step)])
            total = total + r
            step *= 2
    answer = yield jnp.where(first, total + mine, total), perm(swap)
    kept = jnp.where(first, total, total + got)
    return jnp.concatenate([jnp.where(low, kept, answer), jnp.where(low, answer, kept)], axis=0)


def drive(makers, pieces):
    live, done, behind, stage = {}, {}, (), 0
    while live or stage < max(len(makers), len(pieces)):
        if stage < len(makers):
            scan = makers[stage]()
            live[stage] = (scan, next(scan))
        order = sorted(live)
        operands = [live[i][1][0] for i in order]
        tied = lax.optimization_barrier((*operands, *behind))[: len(operands)] if operands else ()
        arrived = [lax.ppermute(a, "seq", live[i][1][1]) for a, i in zip(tied, order)]
        behind = pieces[stage](tied, done) if stage < len(pieces) else ()
        for i, r in zip(order, arrived):
            try:
                live[i] = (live[i][0], live[i][0].send(r))
            except StopIteration as stop:
                done[i] = stop.value
                del live[i]
        stage += 1
    return done


def after(tied, *arrays):
    return lax.optimization_barrier((*arrays, *tied))[: len(arrays)]


def head_sum(a, size):
    if size & (size - 1):
        return lax.psum(a, "head")
    step = 1
    while step < size:
        a = a + lax.ppermute(a, "head", [(i, i ^ step) for i in range(size)])
        step *= 2
    return a


def body(seq_size, head_size, queries, keys, values, gain, out_grad):
    rows, width = queries.shape
    blocks, heads = rows // BLOCK, width // HEAD_DIM
    half = heads // 2
    part = half * HEAD_DIM
    own = lax.axis_index("seq")
    gain = gain.reshape(1, width)
    unit = 2 * rows * HEAD_DIM * HEAD_DIM
    state = (half, HEAD_DIM, HEAD_DIM)
    ks, vs, ts, ws, atts, sums, grads, backs = ({} for _ in range(8))

    def make_state(i):
        ks[i], vs[i], ts[i] = call(
            functools.partial(state_kernel, i * half, half),
            [keys, values],
            [((rows, part), BF16), ((rows, part), BF16), (state, F32)],
            in_specs=[HBM, HBM],
            scratch=[pltpu.SemaphoreType.DMA((2, half))],
            flops=unit * half,
        )

    def make_local(i, tied):
        (k,) = after(tied, ks[i])
        ws[i], atts[i] = call(
            functools.partial(local_kernel, i * half, half, blocks),
            [queries, k, vs[i]],
            [((rows, part), BF16), ((rows, part), F32)],
            scratch=[pltpu.VMEM((rows, HEAD_DIM), BF16)],
            flops=4 * unit * half,
        )
        return ws[i], atts[i]

    def make_stats(i, prefix):
        atts[i], sums[i] = call(
            functools.partial(stats_kernel, i * half, half, blocks),
            [atts[i], queries, prefix, out_grad, gain],
            [((rows, part), F32), ((2, rows), F32)],
            aliases={0: 0},
            flops=unit * half,
        )

    make_state(0)

    def piece_state(tied, done):
        make_state(1)
        return (ts[1],)

    def piece_stats(tied, done):
        make_stats(0, done[0])
        return ()

    prefixes = drive(
        [lambda i=i: scan_stages(ts[i], seq_size, own, False) for i in range(2)],
        [
            piece_state,
            lambda tied, done: make_local(0, tied),
            lambda tied, done: make_local(1, tied),
        ],
    )
    make_stats(0, prefixes[0])
    make_stats(1, prefixes[1])
    total = head_sum(sums[0] + sums[1], head_size)
    inverse, coef = call(functools.partial(factor_kernel, blocks), [total], [((rows, BLOCK), F32)] * 2)

    def make_grad(i):
        grads[i], backs[i] = call(
            functools.partial(grad_kernel, i * half, half),
            [atts[i], queries, out_grad, gain, inverse, coef],
            [((rows, part), BF16), (state, F32)],
            flops=unit * half,
        )

    made = {"query": None}
    locals_ = {}
    size = max(1, half // 2)
    count = half // size

    def make_back(i, j, tied):
        (g,) = after(tied, grads[i])
        first, inner = i * half + j * size, j * size
        ins = [queries, ks[i], vs[i], ws[i], g, prefixes[i]]
        specs, aliases = [VMEM] * len(ins), {}
        if made["query"] is not None:
            aliases = {len(ins): 0}
            ins.append(made["query"])
            specs.append(HBM)
        made["query"], kl, vl = call(
            functools.partial(back_kernel, first, inner, size, blocks),
            ins,
            [((rows, width), BF16), ((rows, size * HEAD_DIM), F32), ((rows, size * HEAD_DIM), F32)],
            in_specs=specs,
            out_specs=[HBM, VMEM, VMEM],
            scratch=[pltpu.VMEM((rows, size * HEAD_DIM), BF16)]
            + [pltpu.VMEM((rows, HEAD_DIM), BF16)] * 3
            + [pltpu.SemaphoreType.DMA((size,))],
            aliases=aliases,
            flops=9 * unit * size,
        )
        locals_[i, j] = (kl, vl)
        return kl, vl

    def make_mixed(tied):
        (inv,) = after(tied, inverse)
        (made["mixed"],) = call(
            functools.partial(mixed_kernel, 2, half), [atts[0], atts[1], gain, inv], [((rows, width), BF16)]
        )
        return (made["mixed"],)

    def make_last(i, suffix):
        ins = [ks[i], vs[i], suffix]
        ins += [locals_[i, j][0] for j in range(count)] + [locals_[i, j][1] for j in range(count)]
        specs, aliases = [VMEM] * len(ins), {}
        if "key" in made:
            aliases = {len(ins): 0, len(ins) + 1: 1}
            ins += [made["key"], made["value"]]
            specs += [HBM, HBM]
        made["key"], made["value"] = call(
            functools.partial(last_kernel, i * half, count, size),
            ins,
            [((rows, width), BF16)] * 2,
            in_specs=specs,
            out_specs=[HBM, HBM],
            scratch=[pltpu.VMEM((rows, part), BF16)] * 2 + [pltpu.SemaphoreType.DMA((2, half))],
            aliases=aliases,
            flops=2 * unit * half,
            vmem=8,
        )
        return ()

    make_grad(0)

    def piece_grad(tied, done):
        make_grad(1)
        return (backs[1],)

    work = [functools.partial(make_back, i, j) for i in range(2) for j in range(count)]
    suffixes = drive(
        [lambda i=i: scan_stages(backs[i], seq_size, own, True) for i in range(2)],
        [piece_grad] + [lambda tied, done, w=w: w(tied) for w in work],
    )
    make_mixed(())
    make_last(0, suffixes[0])
    make_last(1, suffixes[1])
    return made["mixed"], made["query"], made["key"], made["value"]


def solution(mesh):
    placed = (P("seq", "head"), P("seq", "head"), P("seq", "head"), P("head"), P("seq", "head"))
    return jax.shard_map(
        functools.partial(body, mesh.shape["seq"], mesh.shape["head"]),
        mesh=mesh,
        in_specs=placed,
        out_specs=(P("seq", "head"),) * 4,
        check_vma=False,
    )
```

```python
import functools

import jax
import jax.numpy as jnp
from jax import lax
from jax.experimental import pallas as pl
from jax.experimental.pallas import tpu as pltpu
from jax.sharding import PartitionSpec as P

HEAD_DIM = 128
BLOCK = 128
WIDTH = 4096
epsilon = 1e-05

F32 = jnp.float32
BF16 = jnp.bfloat16
VMEM = pl.BlockSpec(memory_space=pltpu.VMEM)
HBM = pl.BlockSpec(memory_space=pltpu.HBM)


def dot(a, b, ca, cb):
    return lax.dot_general(a, b, (((ca,), (cb,)), ((), ())), preferred_element_type=F32)


def causal_mask():
    row = lax.broadcasted_iota(jnp.int32, (BLOCK, BLOCK), 0)
    col = lax.broadcasted_iota(jnp.int32, (BLOCK, BLOCK), 1)
    return col <= row


def rows_of(n):
    return slice(n * BLOCK, (n + 1) * BLOCK)


def cols_of(h):
    return slice(h * HEAD_DIM, (h + 1) * HEAD_DIM)


def cols_at(h):
    return pl.ds(pl.multiple_of(h * HEAD_DIM, HEAD_DIM), HEAD_DIM)


def load_kernel(first, heads, k_hbm, v_hbm, k_ref, v_ref, t_ref, sems):
    copies = []
    for h in range(k_ref.shape[1] // HEAD_DIM):
        for i, (src, dst) in enumerate(((k_hbm, k_ref), (v_hbm, v_ref))):
            copies.append(pltpu.make_async_copy(src.at[:, cols_of(h)], dst.at[:, cols_of(h)], sems.at[i, h]))
            copies[-1].start()
    for h, (k_copy, v_copy) in enumerate(zip(copies[::2], copies[1::2])):
        k_copy.wait()
        v_copy.wait()
        if h < heads:
            t_ref[h] = dot(k_ref[:, cols_of(h)], v_ref[:, cols_of(h)], 0, 0)


def state_kernel(first, heads, k_ref, v_ref, t_ref):
    for h in range(heads):
        t_ref[h] = dot(k_ref[:, cols_of(first + h)], v_ref[:, cols_of(first + h)], 0, 0)


def local_kernel(first, heads, blocks, q_ref, k_ref, v_ref, w_ref, a_ref, low):
    causal = causal_mask()

    def head(h, carry):
        c, cq = cols_at(h), cols_at(h + first)
        for n in range(0, blocks, 2):
            if n + 1 < blocks:
                both = slice(n * BLOCK, (n + 2) * BLOCK)
                s = dot(q_ref[both, cq], k_ref[both, cq], 1, 1)
                w_ref[rows_of(n), c] = jnp.where(causal, s[:BLOCK, :BLOCK], 0.0).astype(BF16)
                w_ref[rows_of(n + 1), c] = jnp.where(causal, s[BLOCK:, BLOCK:], 0.0).astype(BF16)
            else:
                s = dot(q_ref[rows_of(n), cq], k_ref[rows_of(n), cq], 1, 1)
                w_ref[rows_of(n), c] = jnp.where(causal, s, 0.0).astype(BF16)
        prefix = None
        for n in range(blocks - 1):
            s = dot(k_ref[rows_of(n), cq], v_ref[rows_of(n), cq], 0, 0)
            prefix = s if prefix is None else prefix + s
            low[rows_of(n), :] = prefix.astype(BF16)
        a_ref[rows_of(0), c] = dot(w_ref[rows_of(0), c], v_ref[rows_of(0), cq], 1, 0)
        for n in range(1, blocks):
            left = jnp.concatenate([w_ref[rows_of(n), c], q_ref[rows_of(n), cq]], axis=1)
            right = jnp.concatenate([v_ref[rows_of(n), cq], low[rows_of(n - 1), :]], axis=0)
            a_ref[rows_of(n), c] = dot(left, right, 1, 0)
        return carry

    lax.fori_loop(0, heads, head, 0, unroll=min(2, heads))


def stats_kernel(first, parts, size, blocks, *refs):
    a_ins, (q_ref, p_ref, og_ref, gain_ref, a_ref, s_ref) = refs[:parts], refs[parts:]
    low = [p_ref[h].astype(BF16) for h in range(parts * size)]
    for n in range(blocks):
        r = rows_of(n)
        squares = dots = None
        for h in range(parts * size):
            c, cq = cols_of(h), cols_of(first + h)
            att = a_ins[h // size][r, cols_of(h % size)] + dot(q_ref[r, cq], low[h], 1, 0)
            a_ref[r, c] = att
            scaled = gain_ref[:, cq] * og_ref[r, cq].astype(F32)
            squares = att * att if squares is None else squares + att * att
            dots = scaled * att if dots is None else dots + scaled * att
        s_ref[0:1, r] = jnp.sum(squares.T, axis=0, keepdims=True)
        s_ref[1:2, r] = jnp.sum(dots.T, axis=0, keepdims=True)


def factor_kernel(blocks, s_ref, inv_ref, coef_ref):
    inverse = lax.rsqrt(s_ref[0:1, :] / WIDTH + epsilon)
    factor = inverse * inverse * inverse * s_ref[1:2, :] / WIDTH
    for n in range(blocks):
        inv_ref[rows_of(n), :] = jnp.broadcast_to(inverse[:, rows_of(n)], (BLOCK, BLOCK)).T
        coef_ref[rows_of(n), :] = jnp.broadcast_to(factor[:, rows_of(n)], (BLOCK, BLOCK)).T


def grad_kernel(first, heads, a_ref, q_ref, og_ref, gain_ref, inv_ref, coef_ref, g_ref, t_ref):
    for h in range(heads):
        c, cq = cols_of(h), cols_of(first + h)
        scaled = gain_ref[:, cq] * og_ref[:, cq].astype(F32)
        grad = (inv_ref[...] * scaled - coef_ref[...] * a_ref[:, c]).astype(BF16)
        g_ref[:, c] = grad
        t_ref[h] = dot(q_ref[:, cq], grad, 0, 0)


def mixed_kernel(parts, heads, *refs):
    a_refs, (gain_ref, inv_ref, m_ref) = refs[:parts], refs[parts:]
    for p, a_ref in enumerate(a_refs):
        for h in range(heads):
            cq = cols_of(p * heads + h)
            m_ref[:, cq] = (gain_ref[:, cq] * a_ref[:, cols_of(h)] * inv_ref[...]).astype(BF16)


def back_kernel(first, inner, winner, heads, blocks, q_ref, k_ref, v_ref, w_ref, g_ref, p_ref, *rest):
    qg_hbm, kl_ref, vl_ref, qg, bw, plow, slow, sems = rest[-8:]
    causal = causal_mask()

    def copy_out(h, c, cq):
        return pltpu.make_async_copy(qg.at[:, c], qg_hbm.at[:, cq], sems.at[h])

    def head(h, carry):
        c, ci, cw, cq = cols_at(h), cols_at(h + inner), cols_at(h + winner), cols_at(h + first)
        for n in range(blocks):
            r = rows_of(n)
            bw[r, :] = jnp.where(causal, dot(g_ref[r, ci], v_ref[r, cq], 1, 1), 0.0).astype(BF16)
        prefix = p_ref[h + inner]
        plow[rows_of(0), :] = prefix.astype(BF16)
        for n in range(blocks - 1):
            prefix = prefix + dot(k_ref[rows_of(n), cq], v_ref[rows_of(n), cq], 0, 0)
            plow[rows_of(n + 1), :] = prefix.astype(BF16)
        suffix = None
        for n in reversed(range(1, blocks)):
            s = dot(q_ref[rows_of(n), cq], g_ref[rows_of(n), ci], 0, 0)
            suffix = s if suffix is None else suffix + s
            slow[rows_of(n - 1), :] = suffix.astype(BF16)
        for n in range(blocks):
            r = rows_of(n)
            q, k, v, g = q_ref[r, cq], k_ref[r, cq], v_ref[r, cq], g_ref[r, ci]
            qg[r, c] = (dot(bw[r, :], k, 1, 0) + dot(g, plow[r, :], 1, 1)).astype(BF16)
            kp, vp = dot(bw[r, :], q, 0, 0), dot(w_ref[r, cw], g, 0, 0)
            if n + 1 < blocks:
                kp, vp = kp + dot(v, slow[r, :], 1, 1), vp + dot(k, slow[r, :], 1, 0)
            kl_ref[r, c] = kp
            vl_ref[r, c] = vp
        copy_out(h, c, cq).start()
        return carry

    lax.fori_loop(0, heads, head, 0, unroll=min(2, heads))
    for h in range(heads):
        copy_out(h, cols_of(h), cols_of(h + first)).wait()


def last_kernel(first, pieces, heads, k_ref, v_ref, s_ref, *rest):
    kls, vls = rest[:pieces], rest[pieces : 2 * pieces]
    kg_hbm, vg_hbm, kg, vg, sems = rest[-5:]
    copies = []
    for p in range(pieces):
        for i in range(heads):
            h = p * heads + i
            c, cq = cols_of(h), cols_of(first + h)
            low = s_ref[h].astype(BF16)
            kg[:, c] = (kls[p][:, cols_of(i)] + dot(v_ref[:, cq], low, 1, 1)).astype(BF16)
            copies.append(pltpu.make_async_copy(kg.at[:, c], kg_hbm.at[:, cq], sems.at[0, h]))
            copies[-1].start()
            vg[:, c] = (vls[p][:, cols_of(i)] + dot(k_ref[:, cq], low, 1, 0)).astype(BF16)
            copies.append(pltpu.make_async_copy(vg.at[:, c], vg_hbm.at[:, cq], sems.at[1, h]))
            copies[-1].start()
    for copy in copies:
        copy.wait()


def call(kernel, ins, outs, in_specs=None, out_specs=None, scratch=(), aliases=None, flops=0, vmem=6):
    nbytes = sum(a.size * a.dtype.itemsize for a in ins)
    return pl.pallas_call(
        kernel,
        in_specs=in_specs or [VMEM] * len(ins),
        out_specs=tuple(out_specs or [VMEM] * len(outs)),
        out_shape=tuple(jax.ShapeDtypeStruct(shape, dtype) for shape, dtype in outs),
        scratch_shapes=list(scratch),
        input_output_aliases=aliases or {},
        compiler_params=pltpu.CompilerParams(vmem_limit_bytes=vmem << 20),
        cost_estimate=pl.CostEstimate(flops=flops, bytes_accessed=nbytes, transcendentals=0),
    )(*ins)


def scan_stages(states, size, low, reverse):
    place = (lambda i: size - 1 - i) if reverse else (lambda i: i)
    perm = lambda pairs: [(place(i), place(j)) for i, j in pairs]
    outer = size // 2
    swap = [(i, i ^ 1) for i in range(size)]
    at_first = (lambda a, b: jnp.where(low, b, a)) if reverse else (lambda a, b: jnp.where(low, a, b))
    half = states.shape[0] // 2
    mine = jnp.where(low, states[:half], states[half:])
    other = jnp.where(low, states[half:], states[:half])
    got = yield other, perm(swap)
    pair = mine + got
    total = None
    if outer <= 4:
        running = pair
        for hop in range(outer - 1):
            r = yield running, perm([(2 * hop, 2 * hop + 2), (2 * hop + 1, 2 * hop + 3)])
            total = r if total is None else total + r
            running = r + pair
    else:
        total = yield pair, perm([(i, i + 2) for i in range(size - 2)])
        step = 1
        while step < outer - 1:
            r = yield total, perm([(i, i + 2 * step) for i in range(size - 2 * step)])
            total = total + r
            step *= 2
    answer = yield at_first(total + mine, total), perm(swap)
    kept = at_first(total, total + got)
    return jnp.concatenate([jnp.where(low, kept, answer), jnp.where(low, answer, kept)], axis=0)


def drive(makers, pieces, finish):
    live, arrived, behind, settled, event = [], [], (), (), 0
    waiting = list(makers)
    while waiting or live:
        if waiting:
            scan = waiting.pop(0)()
            name, request = len(makers) - len(waiting) - 1, next(scan)
        else:
            name, scan, result = live.pop(0)
            if settled:
                result = after(settled, result)[0]
            try:
                request = scan.send(result)
            except StopIteration as stop:
                settled = finish(name, stop.value)
                continue
        ordered = arrived[-len(makers) - 1 : -len(makers)]
        operand, *_ = lax.optimization_barrier((request[0], *ordered, *behind))
        arrived.append(lax.ppermute(operand, "seq", request[1]))
        live.append((name, scan, arrived[-1]))
        behind = pieces[event]((operand,)) if event < len(pieces) else ()
        event += 1
    for piece in pieces[event:]:
        piece(())


def after(tied, *arrays):
    return lax.optimization_barrier((*arrays, *tied))[: len(arrays)]


def head_sum(a, size):
    if size & (size - 1):
        return lax.psum(a, "head")
    step = 1
    while step < size:
        a = a + lax.ppermute(a, "head", [(i, i ^ step) for i in range(size)])
        step *= 2
    return a


def body(seq_size, head_size, queries, keys, values, gain, out_grad):
    rows, width = queries.shape
    blocks, heads = rows // BLOCK, width // HEAD_DIM
    half = heads // 2
    part = half * HEAD_DIM
    low = lax.axis_index("seq") % 2 == 0
    gain = gain.reshape(1, width)
    unit = 2 * rows * HEAD_DIM * HEAD_DIM
    whole = ((rows, width), BF16)
    state = ((half, HEAD_DIM, HEAD_DIM), F32)

    k, v, t0 = call(
        functools.partial(load_kernel, 0, half),
        [keys, values],
        [whole, whole, state],
        in_specs=[HBM, HBM],
        scratch=[pltpu.SemaphoreType.DMA((2, heads))],
        flops=unit * half,
        vmem=48,
    )
    states = [t0]

    def piece_state(tied):
        (kt,) = after(tied, k)
        states.extend(call(functools.partial(state_kernel, half, half), [kt, v], [state], flops=unit * half))
        return (states[1],)

    size = min(2, half)
    weights, attended = {}, {}

    def piece_local(first, tied):
        (qt,) = after(tied, queries)
        weights[first], attended[first] = call(
            functools.partial(local_kernel, first, size, blocks),
            [qt, k, v],
            [((rows, size * HEAD_DIM), BF16), ((rows, size * HEAD_DIM), F32)],
            scratch=[pltpu.VMEM((rows, HEAD_DIM), BF16)],
            flops=4 * unit * size,
        )
        return weights[first], attended[first]

    prefixes, atts, sums = [], [], []

    def make_stats(i, prefix):
        parts = [attended[first] for first in range(i * half, (i + 1) * half, size)]
        att, s = call(
            functools.partial(stats_kernel, i * half, len(parts), size, blocks),
            [*parts, queries, prefix, out_grad, gain],
            [((rows, part), F32), ((2, rows), F32)],
            flops=unit * half,
        )
        prefixes.append(prefix)
        atts.append(att)
        sums.append(s)
        return att, s

    drive(
        [lambda i=i: scan_stages(states[i], seq_size, low, False) for i in range(2)],
        [piece_state] + [functools.partial(piece_local, first) for first in range(0, heads, size)],
        make_stats,
    )
    total = head_sum(sums[0] + sums[1], head_size)
    inverse, coef = call(functools.partial(factor_kernel, blocks), [total], [((rows, BLOCK), F32)] * 2)

    grads, backs = [], []

    def piece_grad(i, tied):
        (qt,) = after(tied, queries)
        grad, back = call(
            functools.partial(grad_kernel, i * half, half),
            [atts[i], qt, out_grad, gain, inverse, coef],
            [((rows, part), BF16), state],
            flops=unit * half,
        )
        grads.append(grad)
        backs.append(back)
        return (back,)

    made, inner = {}, {}

    def piece_back(h, tied):
        i = h // half
        (qt,) = after(tied, queries)
        ins = [qt, k, v, weights[h // size * size], grads[i], prefixes[i]]
        specs, aliases = [VMEM] * len(ins), {}
        if "query" in made:
            aliases = {len(ins): 0}
            ins.append(made["query"])
            specs.append(HBM)
        made["query"], kl, vl = call(
            functools.partial(back_kernel, h, h % half, h % size, 1, blocks),
            ins,
            [whole, ((rows, HEAD_DIM), F32), ((rows, HEAD_DIM), F32)],
            in_specs=specs,
            out_specs=[HBM, VMEM, VMEM],
            scratch=[pltpu.VMEM((rows, HEAD_DIM), BF16)] * 4 + [pltpu.SemaphoreType.DMA((1,))],
            aliases=aliases,
            flops=9 * unit,
        )
        inner[h] = (kl, vl)
        return kl, vl

    def piece_mixed(tied):
        (inv,) = after(tied, inverse)
        (made["mixed"],) = call(functools.partial(mixed_kernel, 2, half), [*atts, gain, inv], [whole])
        return (made["mixed"],)

    def make_last(i, suffix):
        mine = [inner[h] for h in range(i * half, (i + 1) * half)]
        ins = [k, v, suffix] + [kl for kl, _ in mine] + [vl for _, vl in mine]
        specs, aliases = [VMEM] * len(ins), {}
        if "key" in made:
            aliases = {len(ins): 0, len(ins) + 1: 1}
            ins += [made["key"], made["value"]]
            specs += [HBM, HBM]
        made["key"], made["value"] = call(
            functools.partial(last_kernel, i * half, half, 1),
            ins,
            [whole, whole],
            in_specs=specs,
            out_specs=[HBM, HBM],
            scratch=[pltpu.VMEM((rows, part), BF16)] * 2 + [pltpu.SemaphoreType.DMA((2, half))],
            aliases=aliases,
            flops=2 * unit * half,
        )
        return made["key"], made["value"]

    piece_grad(0, ())
    drive(
        [lambda i=i: scan_stages(backs[i], seq_size, low, True) for i in range(2)],
        [functools.partial(piece_grad, 1)]
        + [functools.partial(piece_back, h) for h in range(heads)]
        + [piece_mixed],
        make_last,
    )
    return made["mixed"], made["query"], made["key"], made["value"]


def solution(mesh):
    placed = (P("seq", "head"), P("seq", "head"), P("seq", "head"), P("head"), P("seq", "head"))
    return jax.shard_map(
        functools.partial(body, mesh.shape["seq"], mesh.shape["head"]),
        mesh=mesh,
        in_specs=placed,
        out_specs=(P("seq", "head"),) * 4,
        check_vma=False,
    )
```

```python
import functools

import jax
import jax.numpy as jnp
from jax import lax
from jax.experimental import pallas as pl
from jax.experimental.pallas import tpu as pltpu
from jax.sharding import PartitionSpec as P

HEAD_DIM = 128
BLOCK = 128
WIDTH = 4096
epsilon = 1e-05

F32 = jnp.float32
BF16 = jnp.bfloat16
VMEM = pl.BlockSpec(memory_space=pltpu.VMEM)
HBM = pl.BlockSpec(memory_space=pltpu.HBM)


def dot(a, b, ca, cb):
    return lax.dot_general(a, b, (((ca,), (cb,)), ((), ())), preferred_element_type=F32)


def causal_mask():
    row = lax.broadcasted_iota(jnp.int32, (BLOCK, BLOCK), 0)
    col = lax.broadcasted_iota(jnp.int32, (BLOCK, BLOCK), 1)
    return col <= row


def rows_of(n):
    return slice(n * BLOCK, (n + 1) * BLOCK)


def cols_of(h):
    return slice(h * HEAD_DIM, (h + 1) * HEAD_DIM)


def cols_at(h):
    return pl.ds(pl.multiple_of(h * HEAD_DIM, HEAD_DIM), HEAD_DIM)


def load_kernel(first, heads, k_hbm, v_hbm, k_ref, v_ref, t_ref, sems):
    copies = []
    for h in range(k_ref.shape[1] // HEAD_DIM):
        for i, (src, dst) in enumerate(((k_hbm, k_ref), (v_hbm, v_ref))):
            copies.append(pltpu.make_async_copy(src.at[:, cols_of(h)], dst.at[:, cols_of(h)], sems.at[i, h]))
            copies[-1].start()
    for h, (k_copy, v_copy) in enumerate(zip(copies[::2], copies[1::2])):
        k_copy.wait()
        v_copy.wait()
        if h < heads:
            t_ref[h] = dot(k_ref[:, cols_of(h)], v_ref[:, cols_of(h)], 0, 0)


def state_kernel(first, heads, k_ref, v_ref, t_ref):
    for h in range(heads):
        t_ref[h] = dot(k_ref[:, cols_of(first + h)], v_ref[:, cols_of(first + h)], 0, 0)


def local_kernel(first, heads, blocks, q_ref, k_ref, v_ref, w_ref, a_ref, low):
    causal = causal_mask()

    def head(h, carry):
        c, cq = cols_at(h), cols_at(h + first)
        for n in range(0, blocks, 2):
            if n + 1 < blocks:
                both = slice(n * BLOCK, (n + 2) * BLOCK)
                s = dot(q_ref[both, cq], k_ref[both, cq], 1, 1)
                w_ref[rows_of(n), c] = jnp.where(causal, s[:BLOCK, :BLOCK], 0.0).astype(BF16)
                w_ref[rows_of(n + 1), c] = jnp.where(causal, s[BLOCK:, BLOCK:], 0.0).astype(BF16)
            else:
                s = dot(q_ref[rows_of(n), cq], k_ref[rows_of(n), cq], 1, 1)
                w_ref[rows_of(n), c] = jnp.where(causal, s, 0.0).astype(BF16)
        prefix = None
        for n in range(blocks - 1):
            s = dot(k_ref[rows_of(n), cq], v_ref[rows_of(n), cq], 0, 0)
            prefix = s if prefix is None else prefix + s
            low[rows_of(n), :] = prefix.astype(BF16)
        a_ref[rows_of(0), c] = dot(w_ref[rows_of(0), c], v_ref[rows_of(0), cq], 1, 0)
        for n in range(1, blocks):
            left = jnp.concatenate([w_ref[rows_of(n), c], q_ref[rows_of(n), cq]], axis=1)
            right = jnp.concatenate([v_ref[rows_of(n), cq], low[rows_of(n - 1), :]], axis=0)
            a_ref[rows_of(n), c] = dot(left, right, 1, 0)
        return carry

    lax.fori_loop(0, heads, head, 0, unroll=min(2, heads))


def stats_kernel(first, parts, size, blocks, *refs):
    a_ins, (q_ref, p_ref, og_ref, gain_ref, a_ref, s_ref) = refs[:parts], refs[parts:]
    low = [p_ref[h].astype(BF16) for h in range(parts * size)]
    for n in range(blocks):
        r = rows_of(n)
        squares = dots = None
        for h in range(parts * size):
            c, cq = cols_of(h), cols_of(first + h)
            att = a_ins[h // size][r, cols_of(h % size)] + dot(q_ref[r, cq], low[h], 1, 0)
            a_ref[r, c] = att
            scaled = gain_ref[:, cq] * og_ref[r, cq].astype(F32)
            squares = att * att if squares is None else squares + att * att
            dots = scaled * att if dots is None else dots + scaled * att
        s_ref[0:1, r] = jnp.sum(squares.T, axis=0, keepdims=True)
        s_ref[1:2, r] = jnp.sum(dots.T, axis=0, keepdims=True)


def factor_kernel(blocks, s_ref, inv_ref, coef_ref):
    inverse = lax.rsqrt(s_ref[0:1, :] / WIDTH + epsilon)
    factor = inverse * inverse * inverse * s_ref[1:2, :] / WIDTH
    for n in range(blocks):
        inv_ref[rows_of(n), :] = jnp.broadcast_to(inverse[:, rows_of(n)], (BLOCK, BLOCK)).T
        coef_ref[rows_of(n), :] = jnp.broadcast_to(factor[:, rows_of(n)], (BLOCK, BLOCK)).T


def grad_kernel(first, heads, a_ref, q_ref, og_ref, gain_ref, inv_ref, coef_ref, g_ref, t_ref):
    for h in range(heads):
        c, cq = cols_of(h), cols_of(first + h)
        scaled = gain_ref[:, cq] * og_ref[:, cq].astype(F32)
        grad = (inv_ref[...] * scaled - coef_ref[...] * a_ref[:, c]).astype(BF16)
        g_ref[:, c] = grad
        t_ref[h] = dot(q_ref[:, cq], grad, 0, 0)


def back_kernel(first, inner, heads, blocks, q_ref, k_ref, v_ref, w_ref, g_ref, p_ref, a_ref, gain_ref, inv_ref, *rest):
    m_hbm, qg_hbm, kl_ref, vl_ref, mixed, qg, bw, plow, slow, sems = rest[-10:]
    causal = causal_mask()
    here = [(h, cols_of(h), cols_of(h + inner), cols_of(h + first)) for h in range(heads)]
    copies = []

    def copy_out(i, h, src, dst):
        copies.append(pltpu.make_async_copy(src.at[:, cols_of(h)], dst.at[:, cols_of(h + first)], sems.at[i, h]))
        copies[-1].start()

    for h, c, ci, cq in here:
        mixed[:, c] = (gain_ref[:, cq] * a_ref[:, ci] * inv_ref[...]).astype(BF16)
        copy_out(0, h, mixed, m_hbm)
    for h, c, ci, cq in here:
        for n in range(0, blocks, 2):
            r = slice(n * BLOCK, min(n + 2, blocks) * BLOCK)
            s = dot(g_ref[r, ci], v_ref[r, cq], 1, 1)
            for m in range(n, min(n + 2, blocks)):
                inside = rows_of(m - n)
                bw[rows_of(m), c] = jnp.where(causal, s[inside, inside], 0.0).astype(BF16)
    for h, c, ci, cq in here:
        prefix = p_ref[h + inner].T
        plow[rows_of(0), c] = prefix.astype(BF16)
        for n in range(blocks - 1):
            prefix = prefix + dot(v_ref[rows_of(n), cq], k_ref[rows_of(n), cq], 0, 0)
            plow[rows_of(n + 1), c] = prefix.astype(BF16)
    for h, c, ci, cq in here:
        for n in range(blocks):
            r = rows_of(n)
            left = jnp.concatenate([bw[r, c], g_ref[r, ci]], axis=1)
            right = jnp.concatenate([k_ref[r, cq], plow[r, c]], axis=0)
            qg[r, c] = dot(left, right, 1, 0).astype(BF16)
        copy_out(1, h, qg, qg_hbm)
    for h, c, ci, cq in here:
        suffix = None
        for n in reversed(range(1, blocks)):
            s = dot(g_ref[rows_of(n), ci], q_ref[rows_of(n), cq], 0, 0)
            suffix = s if suffix is None else suffix + s
            slow[rows_of(n - 1), c] = suffix.astype(BF16)
    for h, c, ci, cq in here:
        for n in range(blocks):
            r = rows_of(n)
            q, k, v, g = q_ref[r, cq], k_ref[r, cq], v_ref[r, cq], g_ref[r, ci]
            vp = dot(w_ref[r, c], g, 0, 0)
            if n + 1 < blocks:
                left = jnp.concatenate([bw[r, c].T, v], axis=1)
                right = jnp.concatenate([q, slow[r, c]], axis=0)
                kp = dot(left, right, 1, 0)
                vp = vp + dot(k, slow[r, c], 1, 1)
            else:
                kp = dot(bw[r, c], q, 0, 0)
            kl_ref[r, c] = kp
            vl_ref[r, c] = vp
    for copy in copies:
        copy.wait()


def last_kernel(first, pieces, heads, k_ref, v_ref, s_ref, *rest):
    kls, vls = rest[:pieces], rest[pieces : 2 * pieces]
    kg_hbm, vg_hbm, kg, vg, sems = rest[-5:]
    copies = []
    for p in range(pieces):
        for i in range(heads):
            h = p * heads + i
            c, cq = cols_of(h), cols_of(first + h)
            low = s_ref[h].astype(BF16)
            kg[:, c] = (kls[p][:, cols_of(i)] + dot(v_ref[:, cq], low, 1, 1)).astype(BF16)
            copies.append(pltpu.make_async_copy(kg.at[:, c], kg_hbm.at[:, cq], sems.at[0, h]))
            copies[-1].start()
            vg[:, c] = (vls[p][:, cols_of(i)] + dot(k_ref[:, cq], low, 1, 0)).astype(BF16)
            copies.append(pltpu.make_async_copy(vg.at[:, c], vg_hbm.at[:, cq], sems.at[1, h]))
            copies[-1].start()
    for copy in copies:
        copy.wait()


def call(kernel, ins, outs, in_specs=None, out_specs=None, scratch=(), aliases=None, flops=0, vmem=6):
    nbytes = sum(a.size * a.dtype.itemsize for a in ins)
    return pl.pallas_call(
        kernel,
        in_specs=in_specs or [VMEM] * len(ins),
        out_specs=tuple(out_specs or [VMEM] * len(outs)),
        out_shape=tuple(jax.ShapeDtypeStruct(shape, dtype) for shape, dtype in outs),
        scratch_shapes=list(scratch),
        input_output_aliases=aliases or {},
        compiler_params=pltpu.CompilerParams(vmem_limit_bytes=vmem << 20),
        cost_estimate=pl.CostEstimate(flops=flops, bytes_accessed=nbytes, transcendentals=0),
    )(*ins)


def scan_stages(states, size, low, reverse):
    place = (lambda i: size - 1 - i) if reverse else (lambda i: i)
    perm = lambda pairs: [(place(i), place(j)) for i, j in pairs]
    outer = size // 2
    swap = [(i, i ^ 1) for i in range(size)]
    at_first = (lambda a, b: jnp.where(low, b, a)) if reverse else (lambda a, b: jnp.where(low, a, b))
    half = states.shape[0] // 2
    mine = jnp.where(low, states[:half], states[half:])
    other = jnp.where(low, states[half:], states[:half])
    got = yield other, perm(swap), False
    pair = mine + got
    total = None
    if outer == 4 and not reverse:
        r = yield pair, perm([(0, 2), (1, 3), (4, 6), (5, 7)]), False
        both = pair + r
        far = yield both, perm([(2, 6), (3, 7)]), False
        (both,) = after((far,), both)
        total = r + far + (yield both, perm([(2, 4), (3, 5)]), True)
    elif outer <= 4:
        running = pair
        for hop in range(outer - 1):
            r = yield running, perm([(2 * hop, 2 * hop + 2), (2 * hop + 1, 2 * hop + 3)]), False
            total = r if total is None else total + r
            running = r + pair
    else:
        total = yield pair, perm([(i, i + 2) for i in range(size - 2)]), False
        step = 1
        while step < outer - 1:
            r = yield total, perm([(i, i + 2 * step) for i in range(size - 2 * step)]), False
            total = total + r
            step *= 2
    answer = yield at_first(total + mine, total), perm(swap), False
    kept = at_first(total, total + got)
    return jnp.concatenate([jnp.where(low, kept, answer), jnp.where(low, answer, kept)], axis=0)


def drive(makers, pieces, finish):
    live, arrived, behind, settled, event = [], [], (), (), 0
    waiting = list(makers)
    while waiting or live:
        if waiting:
            scan = waiting.pop(0)()
            name, request = len(makers) - len(waiting) - 1, next(scan)
        else:
            name, scan, result = live.pop(0)
            if settled:
                result = after(settled, result)[0]
            try:
                request = scan.send(result)
            except StopIteration as stop:
                settled = finish(name, stop.value)
                continue
        back = 1 + name if request[2] else 1 + len(makers)
        ordered = arrived[-back:][:1] if len(arrived) >= back else []
        operand, *_ = lax.optimization_barrier((request[0], *ordered, *behind))
        arrived.append(lax.ppermute(operand, "seq", request[1]))
        live.append((name, scan, arrived[-1]))
        behind = pieces.pop(event)((operand,)) if event in pieces else ()
        event += 1
    for piece in pieces.values():
        piece(())


def after(tied, *arrays):
    return lax.optimization_barrier((*arrays, *tied))[: len(arrays)]


def head_sum(a, size):
    if size & (size - 1):
        return lax.psum(a, "head")
    step = 1
    while step < size:
        a = a + lax.ppermute(a, "head", [(i, i ^ step) for i in range(size)])
        step *= 2
    return a


def body(seq_size, head_size, queries, keys, values, gain, out_grad):
    rows, width = queries.shape
    blocks, heads = rows // BLOCK, width // HEAD_DIM
    half = heads // 2
    part = half * HEAD_DIM
    low = lax.axis_index("seq") % 2 == 0
    gain = gain.reshape(1, width)
    unit = 2 * rows * HEAD_DIM * HEAD_DIM
    whole = ((rows, width), BF16)
    state = ((half, HEAD_DIM, HEAD_DIM), F32)

    k, v, t0 = call(
        functools.partial(load_kernel, 0, half),
        [keys, values],
        [whole, whole, state],
        in_specs=[HBM, HBM],
        scratch=[pltpu.SemaphoreType.DMA((2, heads))],
        flops=unit * half,
        vmem=48,
    )
    states = [t0]

    def piece_state(tied):
        (kt,) = after(tied, k)
        states.extend(call(functools.partial(state_kernel, half, half), [kt, v], [state], flops=unit * half))
        return (states[1], *piece_local(0, (states[1],)))

    size = min(2, half)
    weights, attended = {}, {}

    def piece_local(first, tied):
        (qt,) = after(tied, queries)
        weights[first], attended[first] = call(
            functools.partial(local_kernel, first, size, blocks),
            [qt, k, v],
            [((rows, size * HEAD_DIM), BF16), ((rows, size * HEAD_DIM), F32)],
            scratch=[pltpu.VMEM((rows, HEAD_DIM), BF16)],
            flops=4 * unit * size,
        )
        return weights[first], attended[first]

    prefixes, atts, sums = [], [], []

    def make_stats(i, prefix):
        parts = [attended[first] for first in range(i * half, (i + 1) * half, size)]
        att, s = call(
            functools.partial(stats_kernel, i * half, len(parts), size, blocks),
            [*parts, queries, prefix, out_grad, gain],
            [((rows, part), F32), ((2, rows), F32)],
            flops=unit * half,
        )
        prefixes.append(prefix)
        atts.append(att)
        sums.append(s)
        return att, s

    drive(
        [lambda i=i: scan_stages(states[i], seq_size, low, False) for i in range(2)],
        {0: piece_state, **{2 * i: functools.partial(piece_local, i * size) for i in range(1, heads // size)}},
        make_stats,
    )
    total = head_sum(sums[0] + sums[1], head_size)
    inverse, coef = call(functools.partial(factor_kernel, blocks), [total], [((rows, BLOCK), F32)] * 2)

    grads, backs = [], []

    def piece_grad(i, tied):
        (qt,) = after(tied, queries)
        grad, back = call(
            functools.partial(grad_kernel, i * half, half),
            [atts[i], qt, out_grad, gain, inverse, coef],
            [((rows, part), BF16), state],
            flops=unit * half,
        )
        grads.append(grad)
        backs.append(back)
        return (back,)

    made, inner = {}, {}

    def piece_back(first, tied):
        i = first // half
        (qt,) = after(tied, queries)
        ins = [qt, k, v, weights[first], grads[i], prefixes[i], atts[i], gain, inverse]
        specs, aliases = [VMEM] * len(ins), {}
        if "query" in made:
            aliases = {len(ins): 0, len(ins) + 1: 1}
            ins += [made["mixed"], made["query"]]
            specs += [HBM, HBM]
        own = ((rows, size * HEAD_DIM), F32)
        made["mixed"], made["query"], kl, vl = call(
            functools.partial(back_kernel, first, first % half, size, blocks),
            ins,
            [whole, whole, own, own],
            in_specs=specs,
            out_specs=[HBM, HBM, VMEM, VMEM],
            scratch=[pltpu.VMEM((rows, size * HEAD_DIM), BF16)] * 5 + [pltpu.SemaphoreType.DMA((2, size))],
            aliases=aliases,
            flops=9 * unit * size,
        )
        inner[first] = (kl, vl)
        return kl, vl

    def make_last(i, suffix):
        mine = [inner[first] for first in range(i * half, (i + 1) * half, size)]
        ins = [k, v, suffix] + [kl for kl, _ in mine] + [vl for _, vl in mine]
        specs, aliases = [VMEM] * len(ins), {}
        if "key" in made:
            aliases = {len(ins): 0, len(ins) + 1: 1}
            ins += [made["key"], made["value"]]
            specs += [HBM, HBM]
        made["key"], made["value"] = call(
            functools.partial(last_kernel, i * half, len(mine), size),
            ins,
            [whole, whole],
            in_specs=specs,
            out_specs=[HBM, HBM],
            scratch=[pltpu.VMEM((rows, part), BF16)] * 2 + [pltpu.SemaphoreType.DMA((2, half))],
            aliases=aliases,
            flops=2 * unit * half,
        )
        return made["key"], made["value"]

    piece_grad(0, ())
    drive(
        [lambda i=i: scan_stages(backs[i], seq_size, low, True) for i in range(2)],
        {
            0: functools.partial(piece_grad, 1),
            **{2 * i + 2: functools.partial(piece_back, i * size) for i in range(heads // size)},
        },
        make_last,
    )
    return made["mixed"], made["query"], made["key"], made["value"]


def solution(mesh):
    placed = (P("seq", "head"), P("seq", "head"), P("seq", "head"), P("head"), P("seq", "head"))
    return jax.shard_map(
        functools.partial(body, mesh.shape["seq"], mesh.shape["head"]),
        mesh=mesh,
        in_specs=placed,
        out_specs=(P("seq", "head"),) * 4,
        check_vma=False,
    )
```

```python
import functools

import jax
import jax.numpy as jnp
from jax import lax
from jax.experimental import pallas as pl
from jax.experimental.pallas import tpu as pltpu
from jax.sharding import PartitionSpec as P

HEAD_DIM = 128
BLOCK = 128
WIDTH = 4096
epsilon = 1e-05

F32 = jnp.float32
BF16 = jnp.bfloat16
VMEM = pl.BlockSpec(memory_space=pltpu.VMEM)
HBM = pl.BlockSpec(memory_space=pltpu.HBM)


def dot(a, b, ca, cb):
    return lax.dot_general(a, b, (((ca,), (cb,)), ((), ())), preferred_element_type=F32)


def causal_mask():
    row = lax.broadcasted_iota(jnp.int32, (BLOCK, BLOCK), 0)
    col = lax.broadcasted_iota(jnp.int32, (BLOCK, BLOCK), 1)
    return col <= row


def rows_of(n):
    return slice(n * BLOCK, (n + 1) * BLOCK)


def cols_of(h):
    return slice(h * HEAD_DIM, (h + 1) * HEAD_DIM)


def cols_at(h):
    return pl.ds(pl.multiple_of(h * HEAD_DIM, HEAD_DIM), HEAD_DIM)


def load_kernel(first, heads, k_hbm, v_hbm, k_ref, v_ref, t_ref, sems):
    copies = []
    for h in range(k_ref.shape[1] // HEAD_DIM):
        for i, (src, dst) in enumerate(((k_hbm, k_ref), (v_hbm, v_ref))):
            copies.append(pltpu.make_async_copy(src.at[:, cols_of(h)], dst.at[:, cols_of(h)], sems.at[i, h]))
            copies[-1].start()
    for h, (k_copy, v_copy) in enumerate(zip(copies[::2], copies[1::2])):
        k_copy.wait()
        v_copy.wait()
        if h < heads:
            t_ref[h] = dot(k_ref[:, cols_of(h)], v_ref[:, cols_of(h)], 0, 0)


def state_kernel(first, heads, k_ref, v_ref, t_ref):
    for h in range(heads):
        t_ref[h] = dot(k_ref[:, cols_of(first + h)], v_ref[:, cols_of(first + h)], 0, 0)


def local_kernel(first, heads, blocks, q_ref, k_ref, v_ref, w_ref, a_ref, low):
    causal = causal_mask()

    def head(h, carry):
        c, cq = cols_at(h), cols_at(h + first)
        for n in range(0, blocks, 2):
            if n + 1 < blocks:
                both = slice(n * BLOCK, (n + 2) * BLOCK)
                s = dot(q_ref[both, cq], k_ref[both, cq], 1, 1)
                w_ref[rows_of(n), c] = jnp.where(causal, s[:BLOCK, :BLOCK], 0.0).astype(BF16)
                w_ref[rows_of(n + 1), c] = jnp.where(causal, s[BLOCK:, BLOCK:], 0.0).astype(BF16)
            else:
                s = dot(q_ref[rows_of(n), cq], k_ref[rows_of(n), cq], 1, 1)
                w_ref[rows_of(n), c] = jnp.where(causal, s, 0.0).astype(BF16)
        prefix = None
        for n in range(blocks - 1):
            s = dot(k_ref[rows_of(n), cq], v_ref[rows_of(n), cq], 0, 0)
            prefix = s if prefix is None else prefix + s
            low[rows_of(n), :] = prefix.astype(BF16)
        a_ref[rows_of(0), c] = dot(w_ref[rows_of(0), c], v_ref[rows_of(0), cq], 1, 0)
        for n in range(1, blocks):
            left = jnp.concatenate([w_ref[rows_of(n), c], q_ref[rows_of(n), cq]], axis=1)
            right = jnp.concatenate([v_ref[rows_of(n), cq], low[rows_of(n - 1), :]], axis=0)
            a_ref[rows_of(n), c] = dot(left, right, 1, 0)
        return carry

    lax.fori_loop(0, heads, head, 0, unroll=min(2, heads))


def stats_kernel(first, parts, size, blocks, *refs):
    a_ins, (q_ref, p_ref, og_ref, gain_ref, a_ref, s_ref) = refs[:parts], refs[parts:]
    low = [p_ref[h].astype(BF16) for h in range(parts * size)]
    for n in range(blocks):
        r = rows_of(n)
        squares = dots = None
        for h in range(parts * size):
            c, cq = cols_of(h), cols_of(first + h)
            att = a_ins[h // size][r, cols_of(h % size)] + dot(q_ref[r, cq], low[h], 1, 0)
            a_ref[r, c] = att
            scaled = gain_ref[:, cq] * og_ref[r, cq].astype(F32)
            squares = att * att if squares is None else squares + att * att
            dots = scaled * att if dots is None else dots + scaled * att
        s_ref[0:1, r] = jnp.sum(squares.T, axis=0, keepdims=True)
        s_ref[1:2, r] = jnp.sum(dots.T, axis=0, keepdims=True)


def factor_kernel(blocks, s_ref, inv_ref, coef_ref):
    inverse = lax.rsqrt(s_ref[0:1, :] / WIDTH + epsilon)
    factor = inverse * inverse * inverse * s_ref[1:2, :] / WIDTH
    for n in range(blocks):
        inv_ref[rows_of(n), :] = jnp.broadcast_to(inverse[:, rows_of(n)], (BLOCK, BLOCK)).T
        coef_ref[rows_of(n), :] = jnp.broadcast_to(factor[:, rows_of(n)], (BLOCK, BLOCK)).T


def grad_kernel(first, heads, a_ref, q_ref, og_ref, gain_ref, inv_ref, coef_ref, g_ref, t_ref):
    for h in range(heads):
        c, cq = cols_of(h), cols_of(first + h)
        scaled = gain_ref[:, cq] * og_ref[:, cq].astype(F32)
        grad = (inv_ref[...] * scaled - coef_ref[...] * a_ref[:, c]).astype(BF16)
        g_ref[:, c] = grad
        t_ref[h] = dot(q_ref[:, cq], grad, 0, 0)


def back_kernel(first, inner, winner, heads, blocks, q_ref, k_ref, v_ref, w_ref, g_ref, p_ref, a_ref, gain_ref, inv_ref, *rest):
    m_hbm, qg_hbm, kl_ref, vl_ref, mixed, qg, bw, plow, slow, sems = rest[-10:]
    causal = causal_mask()
    here = [(h, cols_of(h), cols_of(h + inner), cols_of(h + first)) for h in range(heads)]
    copies = []

    def copy_out(i, h, src, dst):
        copies.append(pltpu.make_async_copy(src.at[:, cols_of(h)], dst.at[:, cols_of(h + first)], sems.at[i, h]))
        copies[-1].start()

    for h, c, ci, cq in here:
        mixed[:, c] = (gain_ref[:, cq] * a_ref[:, ci] * inv_ref[...]).astype(BF16)
        copy_out(0, h, mixed, m_hbm)
    for h, c, ci, cq in here:
        for n in range(0, blocks, 2):
            r = slice(n * BLOCK, min(n + 2, blocks) * BLOCK)
            s = dot(g_ref[r, ci], v_ref[r, cq], 1, 1)
            for m in range(n, min(n + 2, blocks)):
                inside = rows_of(m - n)
                bw[rows_of(m), c] = jnp.where(causal, s[inside, inside], 0.0).astype(BF16)
    for h, c, ci, cq in here:
        prefix = p_ref[h + inner].T
        plow[rows_of(0), c] = prefix.astype(BF16)
        for n in range(blocks - 1):
            prefix = prefix + dot(v_ref[rows_of(n), cq], k_ref[rows_of(n), cq], 0, 0)
            plow[rows_of(n + 1), c] = prefix.astype(BF16)
    for h, c, ci, cq in here:
        for n in range(blocks):
            r = rows_of(n)
            left = jnp.concatenate([bw[r, c], g_ref[r, ci]], axis=1)
            right = jnp.concatenate([k_ref[r, cq], plow[r, c]], axis=0)
            qg[r, c] = dot(left, right, 1, 0).astype(BF16)
        copy_out(1, h, qg, qg_hbm)
    for h, c, ci, cq in here:
        suffix = None
        for n in reversed(range(1, blocks)):
            s = dot(g_ref[rows_of(n), ci], q_ref[rows_of(n), cq], 0, 0)
            suffix = s if suffix is None else suffix + s
            slow[rows_of(n - 1), c] = suffix.astype(BF16)
    for h, c, ci, cq in here:
        for n in range(blocks):
            r = rows_of(n)
            q, k, v, g = q_ref[r, cq], k_ref[r, cq], v_ref[r, cq], g_ref[r, ci]
            vp = dot(w_ref[r, cols_of(h + winner)], g, 0, 0)
            if n + 1 < blocks:
                left = jnp.concatenate([bw[r, c].T, v], axis=1)
                right = jnp.concatenate([q, slow[r, c]], axis=0)
                kp = dot(left, right, 1, 0)
                vp = vp + dot(k, slow[r, c], 1, 1)
            else:
                kp = dot(bw[r, c], q, 0, 0)
            kl_ref[r, c] = kp
            vl_ref[r, c] = vp
    for copy in copies:
        copy.wait()


def last_kernel(first, pieces, heads, k_ref, v_ref, s_ref, *rest):
    kls, vls = rest[:pieces], rest[pieces : 2 * pieces]
    kg_hbm, vg_hbm, kg, vg, sems = rest[-5:]
    copies = []
    for p in range(pieces):
        for i in range(heads):
            h = p * heads + i
            c, cq = cols_of(h), cols_of(first + h)
            low = s_ref[h].astype(BF16)
            kg[:, c] = (kls[p][:, cols_of(i)] + dot(v_ref[:, cq], low, 1, 1)).astype(BF16)
            copies.append(pltpu.make_async_copy(kg.at[:, c], kg_hbm.at[:, cq], sems.at[0, h]))
            copies[-1].start()
            vg[:, c] = (vls[p][:, cols_of(i)] + dot(k_ref[:, cq], low, 1, 0)).astype(BF16)
            copies.append(pltpu.make_async_copy(vg.at[:, c], vg_hbm.at[:, cq], sems.at[1, h]))
            copies[-1].start()
    for copy in copies:
        copy.wait()


def call(kernel, ins, outs, in_specs=None, out_specs=None, scratch=(), aliases=None, flops=0, vmem=6):
    nbytes = sum(a.size * a.dtype.itemsize for a in ins)
    return pl.pallas_call(
        kernel,
        in_specs=in_specs or [VMEM] * len(ins),
        out_specs=tuple(out_specs or [VMEM] * len(outs)),
        out_shape=tuple(jax.ShapeDtypeStruct(shape, dtype) for shape, dtype in outs),
        scratch_shapes=list(scratch),
        input_output_aliases=aliases or {},
        compiler_params=pltpu.CompilerParams(vmem_limit_bytes=vmem << 20),
        cost_estimate=pl.CostEstimate(flops=flops, bytes_accessed=nbytes, transcendentals=0),
    )(*ins)


def scan_stages(states, size, low, reverse):
    place = (lambda i: size - 1 - i) if reverse else (lambda i: i)
    perm = lambda pairs: [(place(i), place(j)) for i, j in pairs]
    outer = size // 2
    swap = [(i, i ^ 1) for i in range(size)]
    at_first = (lambda a, b: jnp.where(low, b, a)) if reverse else (lambda a, b: jnp.where(low, a, b))
    half = states.shape[0] // 2
    mine = jnp.where(low, states[:half], states[half:])
    other = jnp.where(low, states[half:], states[:half])
    got = yield other, perm(swap)
    pair = mine + got
    total = None
    if outer <= 4:
        running = pair
        for hop in range(outer - 1):
            r = yield running, perm([(2 * hop, 2 * hop + 2), (2 * hop + 1, 2 * hop + 3)])
            total = r if total is None else total + r
            running = r + pair
    else:
        total = yield pair, perm([(i, i + 2) for i in range(size - 2)])
        step = 1
        while step < outer - 1:
            r = yield total, perm([(i, i + 2 * step) for i in range(size - 2 * step)])
            total = total + r
            step *= 2
    answer = yield at_first(total + mine, total), perm(swap)
    kept = at_first(total, total + got)
    return jnp.concatenate([jnp.where(low, kept, answer), jnp.where(low, answer, kept)], axis=0)


def drive(makers, pieces, finish):
    live, behind, event = [], (), 0
    waiting = list(makers)
    while waiting or live:
        if waiting:
            scan = waiting.pop(0)()
            name, (operand, pairs) = len(makers) - len(waiting) - 1, next(scan)
        else:
            name, scan, result = live.pop(0)
            try:
                operand, pairs = scan.send(after(behind, result)[0])
            except StopIteration as stop:
                behind = finish(name, stop.value)
                continue
        live.append((name, scan, lax.ppermute(operand, "seq", pairs)))
        behind = pieces.pop(event)((operand,)) if event in pieces else ()
        event += 1
    for piece in pieces.values():
        piece(())


def after(tied, *arrays):
    return lax.optimization_barrier((*arrays, *tied))[: len(arrays)] if tied else arrays


def head_sum(a, size):
    if size & (size - 1):
        return lax.psum(a, "head")
    step = 1
    while step < size:
        a = a + lax.ppermute(a, "head", [(i, i ^ step) for i in range(size)])
        step *= 2
    return a


def body(seq_size, head_size, queries, keys, values, gain, out_grad):
    rows, width = queries.shape
    blocks, heads = rows // BLOCK, width // HEAD_DIM
    half = heads // 2
    part = half * HEAD_DIM
    low = lax.axis_index("seq") % 2 == 0
    gain = gain.reshape(1, width)
    unit = 2 * rows * HEAD_DIM * HEAD_DIM
    whole = ((rows, width), BF16)
    state = ((half, HEAD_DIM, HEAD_DIM), F32)

    k, v, t0 = call(
        functools.partial(load_kernel, 0, half),
        [keys, values],
        [whole, whole, state],
        in_specs=[HBM, HBM],
        scratch=[pltpu.SemaphoreType.DMA((2, heads))],
        flops=unit * half,
        vmem=48,
    )
    states = [t0]

    def piece_state(tied):
        (kt,) = after(tied, k)
        states.extend(call(functools.partial(state_kernel, half, half), [kt, v], [state], flops=unit * half))
        return (states[1],)

    size = min(2, half)
    weights, attended = {}, {}

    def piece_local(first, tied):
        (qt,) = after(tied, queries)
        weights[first], attended[first] = call(
            functools.partial(local_kernel, first, size, blocks),
            [qt, k, v],
            [((rows, size * HEAD_DIM), BF16), ((rows, size * HEAD_DIM), F32)],
            scratch=[pltpu.VMEM((rows, HEAD_DIM), BF16)],
            flops=4 * unit * size,
        )
        return weights[first], attended[first]

    prefixes, atts, sums = [], [], []

    def make_stats(i, prefix):
        parts = [attended[first] for first in range(i * half, (i + 1) * half, size)]
        att, s = call(
            functools.partial(stats_kernel, i * half, len(parts), size, blocks),
            [*parts, queries, prefix, out_grad, gain],
            [((rows, part), F32), ((2, rows), F32)],
            flops=unit * half,
        )
        prefixes.append(prefix)
        atts.append(att)
        sums.append(s)
        return att, s

    drive(
        [lambda i=i: scan_stages(states[i], seq_size, low, False) for i in range(2)],
        {0: piece_state, **{i + 1: functools.partial(piece_local, i * size) for i in range(heads // size)}},
        make_stats,
    )
    total = head_sum(sums[0] + sums[1], head_size)
    inverse, coef = call(functools.partial(factor_kernel, blocks), [total], [((rows, BLOCK), F32)] * 2)

    grads, backs = [], []

    def piece_grad(i, tied):
        (qt,) = after(tied, queries)
        grad, back = call(
            functools.partial(grad_kernel, i * half, half),
            [atts[i], qt, out_grad, gain, inverse, coef],
            [((rows, part), BF16), state],
            flops=unit * half,
        )
        grads.append(grad)
        backs.append(back)
        return (back,)

    made, inner = {}, {}

    def piece_back(first, tied):
        i = first // half
        (qt,) = after(tied, queries)
        ins = [qt, k, v, weights[first // size * size], grads[i], prefixes[i], atts[i], gain, inverse]
        specs, aliases = [VMEM] * len(ins), {}
        if "query" in made:
            aliases = {len(ins): 0, len(ins) + 1: 1}
            ins += [made["mixed"], made["query"]]
            specs += [HBM, HBM]
        own = ((rows, HEAD_DIM), F32)
        made["mixed"], made["query"], kl, vl = call(
            functools.partial(back_kernel, first, first % half, first % size, 1, blocks),
            ins,
            [whole, whole, own, own],
            in_specs=specs,
            out_specs=[HBM, HBM, VMEM, VMEM],
            scratch=[pltpu.VMEM((rows, HEAD_DIM), BF16)] * 5 + [pltpu.SemaphoreType.DMA((2, 1))],
            aliases=aliases,
            flops=9 * unit,
        )
        inner[first] = (kl, vl)
        return kl, vl

    def make_last(i, suffix):
        mine = [inner[first] for first in range(i * half, (i + 1) * half)]
        ins = [k, v, suffix] + [kl for kl, _ in mine] + [vl for _, vl in mine]
        specs, aliases = [VMEM] * len(ins), {}
        if "key" in made:
            aliases = {len(ins): 0, len(ins) + 1: 1}
            ins += [made["key"], made["value"]]
            specs += [HBM, HBM]
        made["key"], made["value"] = call(
            functools.partial(last_kernel, i * half, half, 1),
            ins,
            [whole, whole],
            in_specs=specs,
            out_specs=[HBM, HBM],
            scratch=[pltpu.VMEM((rows, part), BF16)] * 2 + [pltpu.SemaphoreType.DMA((2, half))],
            aliases=aliases,
            flops=2 * unit * half,
        )
        return made["key"], made["value"]

    piece_grad(0, ())
    drive(
        [lambda i=i: scan_stages(backs[i], seq_size, low, True) for i in range(2)],
        {
            0: functools.partial(piece_grad, 1),
            **{i + 1: functools.partial(piece_back, i) for i in range(heads)},
        },
        make_last,
    )
    return made["mixed"], made["query"], made["key"], made["value"]


def solution(mesh):
    placed = (P("seq", "head"), P("seq", "head"), P("seq", "head"), P("head"), P("seq", "head"))
    return jax.shard_map(
        functools.partial(body, mesh.shape["seq"], mesh.shape["head"]),
        mesh=mesh,
        in_specs=placed,
        out_specs=(P("seq", "head"),) * 4,
        check_vma=False,
    )
```

```python
import functools

import jax
import jax.numpy as jnp
from jax import lax
from jax.experimental import pallas as pl
from jax.experimental.pallas import tpu as pltpu
from jax.sharding import PartitionSpec as P

HEAD_DIM = 128
BLOCK = 128
WIDTH = 4096
epsilon = 1e-05

F32 = jnp.float32
BF16 = jnp.bfloat16
VMEM = pl.BlockSpec(memory_space=pltpu.VMEM)
HBM = pl.BlockSpec(memory_space=pltpu.HBM)


def dot(a, b, ca, cb):
    return lax.dot_general(a, b, (((ca,), (cb,)), ((), ())), preferred_element_type=F32)


def causal_mask():
    row = lax.broadcasted_iota(jnp.int32, (BLOCK, BLOCK), 0)
    col = lax.broadcasted_iota(jnp.int32, (BLOCK, BLOCK), 1)
    return col <= row


def rows_of(n):
    return slice(n * BLOCK, (n + 1) * BLOCK)


def cols_of(h):
    return slice(h * HEAD_DIM, (h + 1) * HEAD_DIM)


def cols_at(h):
    return pl.ds(pl.multiple_of(h * HEAD_DIM, HEAD_DIM), HEAD_DIM)


def load_kernel(first, heads, k_hbm, v_hbm, k_ref, v_ref, t_ref, sems):
    copies = []
    for h in range(heads):
        for i, (src, dst) in enumerate(((k_hbm, k_ref), (v_hbm, v_ref))):
            copies.append(pltpu.make_async_copy(src.at[:, cols_of(first + h)], dst.at[:, cols_of(h)], sems.at[i, h]))
            copies[-1].start()
    for h in range(heads):
        copies[2 * h].wait()
        copies[2 * h + 1].wait()
        t_ref[h] = dot(k_ref[:, cols_of(h)], v_ref[:, cols_of(h)], 0, 0)


def local_kernel(first, inner, heads, blocks, q_ref, k_ref, v_ref, w_ref, a_ref, low):
    causal = causal_mask()

    def head(h, carry):
        c, ci, cq = cols_at(h), cols_at(h + inner), cols_at(h + first)
        for n in range(0, blocks, 2):
            if n + 1 < blocks:
                both = slice(n * BLOCK, (n + 2) * BLOCK)
                s = dot(q_ref[both, cq], k_ref[both, ci], 1, 1)
                w_ref[rows_of(n), c] = jnp.where(causal, s[:BLOCK, :BLOCK], 0.0).astype(BF16)
                w_ref[rows_of(n + 1), c] = jnp.where(causal, s[BLOCK:, BLOCK:], 0.0).astype(BF16)
            else:
                s = dot(q_ref[rows_of(n), cq], k_ref[rows_of(n), ci], 1, 1)
                w_ref[rows_of(n), c] = jnp.where(causal, s, 0.0).astype(BF16)
        prefix = None
        for n in range(blocks - 1):
            s = dot(k_ref[rows_of(n), ci], v_ref[rows_of(n), ci], 0, 0)
            prefix = s if prefix is None else prefix + s
            low[rows_of(n), :] = prefix.astype(BF16)
        a_ref[rows_of(0), c] = dot(w_ref[rows_of(0), c], v_ref[rows_of(0), ci], 1, 0)
        for n in range(1, blocks):
            left = jnp.concatenate([w_ref[rows_of(n), c], q_ref[rows_of(n), cq]], axis=1)
            right = jnp.concatenate([v_ref[rows_of(n), ci], low[rows_of(n - 1), :]], axis=0)
            a_ref[rows_of(n), c] = dot(left, right, 1, 0)
        return carry

    lax.fori_loop(0, heads, head, 0, unroll=min(2, heads))


def stats_kernel(first, parts, size, blocks, *refs):
    a_ins, (q_ref, p_ref, og_ref, gain_ref, a_ref, s_ref) = refs[:parts], refs[parts:]
    low = [p_ref[h].astype(BF16) for h in range(parts * size)]
    for n in range(blocks):
        r = rows_of(n)
        squares = dots = None
        for h in range(parts * size):
            c, cq = cols_of(h), cols_of(first + h)
            att = a_ins[h // size][r, cols_of(h % size)] + dot(q_ref[r, cq], low[h], 1, 0)
            a_ref[r, c] = att
            scaled = gain_ref[:, cq] * og_ref[r, cq].astype(F32)
            squares = att * att if squares is None else squares + att * att
            dots = scaled * att if dots is None else dots + scaled * att
        s_ref[0:1, r] = jnp.sum(squares.T, axis=0, keepdims=True)
        s_ref[1:2, r] = jnp.sum(dots.T, axis=0, keepdims=True)


def grad_kernel(first, heads, blocks, a_ref, q_ref, og_ref, gain_ref, *rest):
    if len(rest) == 5:
        s_ref, g_ref, t_ref, inv_ref, coef_ref = rest
        inverse = lax.rsqrt(s_ref[0:1, :] / WIDTH + epsilon)
        factor = inverse * inverse * inverse * s_ref[1:2, :] / WIDTH
        for n in range(blocks):
            inv_ref[rows_of(n), :] = jnp.broadcast_to(inverse[:, rows_of(n)], (BLOCK, BLOCK)).T
            coef_ref[rows_of(n), :] = jnp.broadcast_to(factor[:, rows_of(n)], (BLOCK, BLOCK)).T
    else:
        inv_ref, coef_ref, g_ref, t_ref = rest
    for h in range(heads):
        c, cq = cols_of(h), cols_of(first + h)
        scaled = gain_ref[:, cq] * og_ref[:, cq].astype(F32)
        grad = (inv_ref[...] * scaled - coef_ref[...] * a_ref[:, c]).astype(BF16)
        g_ref[:, c] = grad
        t_ref[h] = dot(q_ref[:, cq], grad, 0, 0)


def flush(pairs, sems):
    copies = [pltpu.make_async_copy(src, dst, sems.at[i]) for i, (src, dst) in enumerate(pairs)]
    for copy in copies:
        copy.start()
    return copies


def back_kernel(h, inner, winner, blocks, before, q_ref, k_ref, v_ref, w_ref, g_ref, p_ref, a_ref, gain_ref, inv_ref, *rest):
    copies = []
    if before is not None:
        old_m, old_q = rest[:2]
        m_ref, qg_ref, kl_ref, vl_ref, m_hbm, q_hbm, bw, plow, slow, sems = rest[-10:]
        copies = flush([(old_m, m_hbm.at[:, cols_of(before)]), (old_q, q_hbm.at[:, cols_of(before)])], sems)
    else:
        m_ref, qg_ref, kl_ref, vl_ref, bw, plow, slow = rest
    causal = causal_mask()
    ci, cw, cq = cols_of(inner), cols_of(winner), cols_of(h)
    m_ref[...] = (gain_ref[:, cq] * a_ref[:, ci] * inv_ref[...]).astype(BF16)
    for n in range(0, blocks, 2):
        r = slice(n * BLOCK, min(n + 2, blocks) * BLOCK)
        s = dot(g_ref[r, ci], v_ref[r, ci], 1, 1)
        for m in range(n, min(n + 2, blocks)):
            inside = rows_of(m - n)
            bw[rows_of(m), :] = jnp.where(causal, s[inside, inside], 0.0).astype(BF16)
    prefix = p_ref[inner].T
    plow[rows_of(0), :] = prefix.astype(BF16)
    for n in range(blocks - 1):
        prefix = prefix + dot(v_ref[rows_of(n), ci], k_ref[rows_of(n), ci], 0, 0)
        plow[rows_of(n + 1), :] = prefix.astype(BF16)
    suffix = None
    for n in reversed(range(1, blocks)):
        s = dot(g_ref[rows_of(n), ci], q_ref[rows_of(n), cq], 0, 0)
        suffix = s if suffix is None else suffix + s
        slow[rows_of(n - 1), :] = suffix.astype(BF16)
    for n in range(blocks):
        r = rows_of(n)
        q, k, v, g = q_ref[r, cq], k_ref[r, ci], v_ref[r, ci], g_ref[r, ci]
        left = jnp.concatenate([bw[r, :], g], axis=1)
        right = jnp.concatenate([k, plow[r, :]], axis=0)
        qg_ref[r, :] = dot(left, right, 1, 0).astype(BF16)
        vp = dot(w_ref[r, cw], g, 0, 0)
        if n + 1 < blocks:
            left = jnp.concatenate([bw[r, :].T, v], axis=1)
            right = jnp.concatenate([q, slow[r, :]], axis=0)
            kp = dot(left, right, 1, 0)
            vp = vp + dot(k, slow[r, :], 1, 1)
        else:
            kp = dot(bw[r, :], q, 0, 0)
        kl_ref[r, :] = kp
        vl_ref[r, :] = vp
    for copy in copies:
        copy.wait()


def last_kernel(heads, before, k_ref, v_ref, s_ref, *rest):
    kls, vls, rest = rest[:heads], rest[heads : 2 * heads], rest[2 * heads :]
    old_a, old_b = rest[:2]
    if before is not None:
        kg, vg, a_hbm, b_hbm, sems = rest[-5:]
        copies = flush([(old_a, a_hbm.at[:, cols_of(before)]), (old_b, b_hbm.at[:, cols_of(before)])], sems.at[0])
    else:
        a_hbm, b_hbm, kg, vg, sems = rest[-5:]
        there = slice(0, heads * HEAD_DIM)
        copies = flush([(old_a, a_hbm.at[:, there]), (old_b, b_hbm.at[:, there])], sems.at[0])
    for h in range(heads):
        c = cols_of(h)
        low = s_ref[h].astype(BF16)
        kg[:, c] = (kls[h][...] + dot(v_ref[:, c], low, 1, 1)).astype(BF16)
        vg[:, c] = (vls[h][...] + dot(k_ref[:, c], low, 1, 0)).astype(BF16)
        if before is None:
            to = cols_of(heads + h)
            copies += flush([(kg.at[:, c], a_hbm.at[:, to]), (vg.at[:, c], b_hbm.at[:, to])], sems.at[1 + h])
    for copy in copies:
        copy.wait()


def call(kernel, ins, outs, in_specs=None, out_specs=None, scratch=(), aliases=None, flops=0, vmem=6):
    nbytes = sum(a.size * a.dtype.itemsize for a in ins)
    return pl.pallas_call(
        kernel,
        in_specs=in_specs or [VMEM] * len(ins),
        out_specs=tuple(out_specs or [VMEM] * len(outs)),
        out_shape=tuple(jax.ShapeDtypeStruct(shape, dtype) for shape, dtype in outs),
        scratch_shapes=list(scratch),
        input_output_aliases=aliases or {},
        compiler_params=pltpu.CompilerParams(vmem_limit_bytes=vmem << 20),
        cost_estimate=pl.CostEstimate(flops=flops, bytes_accessed=nbytes, transcendentals=0),
    )(*ins)


def scan_stages(states, size, low, reverse):
    place = (lambda i: size - 1 - i) if reverse else (lambda i: i)
    perm = lambda pairs: [(place(i), place(j)) for i, j in pairs]
    outer = size // 2
    swap = [(i, i ^ 1) for i in range(size)]
    at_first = (lambda a, b: jnp.where(low, b, a)) if reverse else (lambda a, b: jnp.where(low, a, b))
    half = states.shape[0] // 2
    mine = jnp.where(low, states[:half], states[half:])
    other = jnp.where(low, states[half:], states[:half])
    got = yield other, perm(swap)
    pair = mine + got
    total = None
    if outer <= 4:
        running = pair
        for hop in range(outer - 1):
            r = yield running, perm([(2 * hop, 2 * hop + 2), (2 * hop + 1, 2 * hop + 3)])
            total = r if total is None else total + r
            running = r + pair
    else:
        total = yield pair, perm([(i, i + 2) for i in range(size - 2)])
        step = 1
        while step < outer - 1:
            r = yield total, perm([(i, i + 2 * step) for i in range(size - 2 * step)])
            total = total + r
            step *= 2
    answer = yield at_first(total + mine, total), perm(swap)
    kept = at_first(total, total + got)
    return jnp.concatenate([jnp.where(low, kept, answer), jnp.where(low, answer, kept)], axis=0)


def drive(makers, pieces, finish):
    live, behind, event = [], (), 0
    waiting = list(makers)
    while waiting or live:
        if waiting:
            scan = waiting.pop(0)()
            name, (operand, pairs) = len(makers) - len(waiting) - 1, next(scan)
        else:
            name, scan, result = live.pop(0)
            try:
                operand, pairs = scan.send(after(behind, result)[0])
            except StopIteration as stop:
                behind = finish(name, stop.value)
                continue
        live.append((name, scan, lax.ppermute(operand, "seq", pairs)))
        behind = pieces.pop(event)((operand,)) if event in pieces else ()
        event += 1
    for piece in pieces.values():
        piece(())


def after(tied, *arrays):
    return lax.optimization_barrier((*arrays, *tied))[: len(arrays)] if tied else arrays


def head_sum(a, size):
    if size & (size - 1):
        return lax.psum(a, "head")
    step = 1
    while step < size:
        a = a + lax.ppermute(a, "head", [(i, i ^ step) for i in range(size)])
        step *= 2
    return a


def body(seq_size, head_size, queries, keys, values, gain, out_grad):
    rows, width = queries.shape
    blocks, heads = rows // BLOCK, width // HEAD_DIM
    half = heads // 2
    part = half * HEAD_DIM
    low = lax.axis_index("seq") % 2 == 0
    gain = gain.reshape(1, width)
    unit = 2 * rows * HEAD_DIM * HEAD_DIM
    whole = ((rows, width), BF16)
    state = ((half, HEAD_DIM, HEAD_DIM), F32)

    ks, vs, states = [], [], []

    def piece_state(i, tied):
        k, v, t = call(
            functools.partial(load_kernel, i * half, half),
            after(tied, keys, values),
            [((rows, part), BF16), ((rows, part), BF16), state],
            in_specs=[HBM, HBM],
            scratch=[pltpu.SemaphoreType.DMA((2, half))],
            flops=unit * half,
            vmem=50,
        )
        ks.append(k)
        vs.append(v)
        states.append(t)
        return (t,)

    piece_state(0, ())

    size = min(2, half)
    weights, attended = {}, {}

    def piece_local(first, tied):
        (qt,) = after(tied, queries)
        weights[first], attended[first] = call(
            functools.partial(local_kernel, first, first % half, size, blocks),
            [qt, ks[first // half], vs[first // half]],
            [((rows, size * HEAD_DIM), BF16), ((rows, size * HEAD_DIM), F32)],
            scratch=[pltpu.VMEM((rows, HEAD_DIM), BF16)],
            flops=4 * unit * size,
        )
        return weights[first], attended[first]

    prefixes, atts, sums = [], [], []

    def make_stats(i, prefix):
        parts = [attended[first] for first in range(i * half, (i + 1) * half, size)]
        att, s = call(
            functools.partial(stats_kernel, i * half, len(parts), size, blocks),
            [*parts, queries, prefix, out_grad, gain],
            [((rows, part), F32), ((2, rows), F32)],
            flops=unit * half,
        )
        prefixes.append(prefix)
        atts.append(att)
        sums.append(s)
        return att, s

    drive(
        [lambda i=i: scan_stages(states[i], seq_size, low, False) for i in range(2)],
        {0: functools.partial(piece_state, 1), **{i + 1: functools.partial(piece_local, i * size) for i in range(heads // size)}},
        make_stats,
    )
    total = head_sum(sums[0] + sums[1], head_size)

    grads, backs, factors = [], [], []

    def piece_grad(i, tied):
        (qt,) = after(tied, queries)
        grad, back, *new = call(
            functools.partial(grad_kernel, i * half, half, blocks),
            [atts[i], qt, out_grad, gain, *(factors or [total])],
            [((rows, part), BF16), state] + ([] if factors else [((rows, BLOCK), F32)] * 2),
            flops=unit * half,
        )
        factors.extend(new)
        grads.append(grad)
        backs.append(back)
        return (back,)

    column = (rows, HEAD_DIM)
    inner, made, fresh = {}, [], []

    def piece_back(h, tied):
        i = h // half
        (qt,) = after(tied, queries)
        ins = [qt, ks[i], vs[i], weights[h // size * size], grads[i], prefixes[i], atts[i], gain, factors[0], *fresh]
        specs, outs, aliases = [VMEM] * len(ins), [(column, BF16)] * 2 + [(column, F32)] * 2, {}
        out_specs, scratch = [VMEM] * 4, [pltpu.VMEM(column, BF16)] * 3
        if fresh:
            aliases = {len(ins) + n: 4 + n for n in range(len(made))}
            ins, specs = ins + made, specs + [HBM] * len(made)
            outs, out_specs = outs + [whole] * 2, out_specs + [HBM] * 2
            scratch.append(pltpu.SemaphoreType.DMA((2,)))
        m, q, *others = call(
            functools.partial(back_kernel, h, h % half, h % size, blocks, h - 1 if fresh else None),
            ins,
            outs,
            in_specs=specs,
            out_specs=out_specs,
            scratch=scratch,
            aliases=aliases,
            flops=9 * unit,
        )
        inner[h], made[:] = others[:2], others[2:]
        fresh[:] = [m, q]
        return tuple(inner[h])

    results = []

    def make_last(i, suffix):
        mine = [inner[h] for h in range(i * half, (i + 1) * half)]
        ins = [ks[i], vs[i], suffix] + [kl for kl, _ in mine] + [vl for _, vl in mine] + (results if i else fresh)
        specs, aliases = [VMEM] * len(ins), {}
        here = [((rows, part), BF16)] * 2
        if i:
            outs, out_specs, scratch = [whole] * 2, [HBM] * 2, [pltpu.VMEM(*pair) for pair in here]
        else:
            aliases = {len(ins) + n: 2 + n for n in range(len(made))}
            ins, specs = ins + made, specs + [HBM] * len(made)
            outs, out_specs, scratch = here + [whole] * 2, [VMEM] * 2 + [HBM] * 2, []
        results.clear()
        got = call(
            functools.partial(last_kernel, half, None if i else heads - 1),
            ins,
            outs,
            in_specs=specs,
            out_specs=out_specs,
            scratch=scratch + [pltpu.SemaphoreType.DMA((1 + half, 2))],
            aliases=aliases,
            flops=2 * unit * half,
        )
        results.extend(got[:2])
        if i == 0:
            made[:] = got[2:]
        return tuple(got)

    piece_grad(0, ())
    drive(
        [lambda i=i: scan_stages(backs[i], seq_size, low, True) for i in range(2)],
        {
            0: functools.partial(piece_grad, 1),
            **{i + 1: functools.partial(piece_back, i) for i in range(heads)},
        },
        make_last,
    )
    return (*made, *results)


def solution(mesh):
    placed = (P("seq", "head"), P("seq", "head"), P("seq", "head"), P("head"), P("seq", "head"))
    return jax.shard_map(
        functools.partial(body, mesh.shape["seq"], mesh.shape["head"]),
        mesh=mesh,
        in_specs=placed,
        out_specs=(P("seq", "head"),) * 4,
        check_vma=False,
    )
```

```python
import functools

import jax
import jax.numpy as jnp
from jax import lax
from jax.experimental import pallas as pl
from jax.experimental.pallas import tpu as pltpu
from jax.sharding import PartitionSpec as P

HEAD_DIM = 128
BLOCK = 128
WIDTH = 4096
epsilon = 1e-05

F32 = jnp.float32
BF16 = jnp.bfloat16
VMEM = pl.BlockSpec(memory_space=pltpu.VMEM)
HBM = pl.BlockSpec(memory_space=pltpu.HBM)


def dot(a, b, ca, cb):
    return lax.dot_general(a, b, (((ca,), (cb,)), ((), ())), preferred_element_type=F32)


def causal_mask():
    row = lax.broadcasted_iota(jnp.int32, (BLOCK, BLOCK), 0)
    col = lax.broadcasted_iota(jnp.int32, (BLOCK, BLOCK), 1)
    return col <= row


def rows_of(n):
    return slice(n * BLOCK, (n + 1) * BLOCK)


def cols_of(h):
    return slice(h * HEAD_DIM, (h + 1) * HEAD_DIM)


def cols_at(h):
    return pl.ds(pl.multiple_of(h * HEAD_DIM, HEAD_DIM), HEAD_DIM)


def load_kernel(first, heads, k_hbm, v_hbm, k_ref, v_ref, t_ref, sems):
    copies = []
    for h in range(heads):
        for i, (src, dst) in enumerate(((k_hbm, k_ref), (v_hbm, v_ref))):
            copies.append(pltpu.make_async_copy(src.at[:, cols_of(first + h)], dst.at[:, cols_of(h)], sems.at[i, h]))
            copies[-1].start()
    for h in range(heads):
        copies[2 * h].wait()
        copies[2 * h + 1].wait()
        t_ref[h] = dot(k_ref[:, cols_of(h)], v_ref[:, cols_of(h)], 0, 0)


def local_kernel(first, inner, heads, blocks, q_ref, k_ref, v_ref, w_ref, a_ref, low):
    causal = causal_mask()

    def head(h, carry):
        c, ci, cq = cols_at(h), cols_at(h + inner), cols_at(h + first)
        for n in range(0, blocks, 2):
            if n + 1 < blocks:
                both = slice(n * BLOCK, (n + 2) * BLOCK)
                s = dot(q_ref[both, cq], k_ref[both, ci], 1, 1)
                w_ref[rows_of(n), c] = jnp.where(causal, s[:BLOCK, :BLOCK], 0.0).astype(BF16)
                w_ref[rows_of(n + 1), c] = jnp.where(causal, s[BLOCK:, BLOCK:], 0.0).astype(BF16)
            else:
                s = dot(q_ref[rows_of(n), cq], k_ref[rows_of(n), ci], 1, 1)
                w_ref[rows_of(n), c] = jnp.where(causal, s, 0.0).astype(BF16)
        prefix = None
        for n in range(blocks - 1):
            s = dot(k_ref[rows_of(n), ci], v_ref[rows_of(n), ci], 0, 0)
            prefix = s if prefix is None else prefix + s
            low[rows_of(n), :] = prefix.astype(BF16)
        a_ref[rows_of(0), c] = dot(w_ref[rows_of(0), c], v_ref[rows_of(0), ci], 1, 0)
        for n in range(1, blocks):
            left = jnp.concatenate([w_ref[rows_of(n), c], q_ref[rows_of(n), cq]], axis=1)
            right = jnp.concatenate([v_ref[rows_of(n), ci], low[rows_of(n - 1), :]], axis=0)
            a_ref[rows_of(n), c] = dot(left, right, 1, 0)
        return carry

    lax.fori_loop(0, heads, head, 0, unroll=min(2, heads))


def stats_kernel(first, parts, size, blocks, *refs):
    a_ins, (q_ref, p_ref, og_ref, gain_ref, a_ref, s_ref) = refs[:parts], refs[parts:]
    low = [p_ref[h].astype(BF16) for h in range(parts * size)]
    for n in range(blocks):
        r = rows_of(n)
        squares = dots = None
        for h in range(parts * size):
            c, cq = cols_of(h), cols_of(first + h)
            att = a_ins[h // size][r, cols_of(h % size)] + dot(q_ref[r, cq], low[h], 1, 0)
            a_ref[r, c] = att
            scaled = gain_ref[:, cq] * og_ref[r, cq].astype(F32)
            squares = att * att if squares is None else squares + att * att
            dots = scaled * att if dots is None else dots + scaled * att
        s_ref[0:1, r] = jnp.sum(squares.T, axis=0, keepdims=True)
        s_ref[1:2, r] = jnp.sum(dots.T, axis=0, keepdims=True)


def grad_kernel(first, heads, blocks, a_ref, q_ref, og_ref, gain_ref, *rest):
    if len(rest) == 5:
        s_ref, g_ref, t_ref, inv_ref, coef_ref = rest
        inverse = lax.rsqrt(s_ref[0:1, :] / WIDTH + epsilon)
        factor = inverse * inverse * inverse * s_ref[1:2, :] / WIDTH
        for n in range(blocks):
            inv_ref[rows_of(n), :] = jnp.broadcast_to(inverse[:, rows_of(n)], (BLOCK, BLOCK)).T
            coef_ref[rows_of(n), :] = jnp.broadcast_to(factor[:, rows_of(n)], (BLOCK, BLOCK)).T
    else:
        inv_ref, coef_ref, g_ref, t_ref = rest
    for h in range(heads):
        c, cq = cols_of(h), cols_of(first + h)
        scaled = gain_ref[:, cq] * og_ref[:, cq].astype(F32)
        grad = (inv_ref[...] * scaled - coef_ref[...] * a_ref[:, c]).astype(BF16)
        g_ref[:, c] = grad
        t_ref[h] = dot(q_ref[:, cq], grad, 0, 0)


def flush(pairs, sems):
    copies = [pltpu.make_async_copy(src, dst, sems.at[i]) for i, (src, dst) in enumerate(pairs)]
    for copy in copies:
        copy.start()
    return copies


def back_kernel(first, heads, inner, winner, blocks, before, q_ref, k_ref, v_ref, w_ref, g_ref, p_ref, a_ref, gain_ref, inv_ref, *rest):
    copies = []
    if before is not None:
        old_m, old_q = rest[:2]
        m_ref, qg_ref, kl_ref, vl_ref, m_hbm, q_hbm, bw, plow, slow, sems = rest[-10:]
        copies = flush([(old_m, m_hbm.at[:, before]), (old_q, q_hbm.at[:, before])], sems)
    else:
        m_ref, qg_ref, kl_ref, vl_ref, bw, plow, slow = rest
    causal = causal_mask()
    here = [(h, cols_of(h), cols_of(h + inner), cols_of(h + winner), cols_of(h + first)) for h in range(heads)]
    for h, c, ci, cw, cq in here:
        m_ref[:, c] = (gain_ref[:, cq] * a_ref[:, ci] * inv_ref[...]).astype(BF16)
    for h, c, ci, cw, cq in here:
        for n in range(0, blocks, 2):
            r = slice(n * BLOCK, min(n + 2, blocks) * BLOCK)
            s = dot(g_ref[r, ci], v_ref[r, ci], 1, 1)
            for m in range(n, min(n + 2, blocks)):
                inside = rows_of(m - n)
                bw[rows_of(m), c] = jnp.where(causal, s[inside, inside], 0.0).astype(BF16)
    for h, c, ci, cw, cq in here:
        prefix = p_ref[h + inner].T
        plow[rows_of(0), c] = prefix.astype(BF16)
        for n in range(blocks - 1):
            prefix = prefix + dot(v_ref[rows_of(n), ci], k_ref[rows_of(n), ci], 0, 0)
            plow[rows_of(n + 1), c] = prefix.astype(BF16)
    for h, c, ci, cw, cq in here:
        suffix = None
        for n in reversed(range(1, blocks)):
            s = dot(g_ref[rows_of(n), ci], q_ref[rows_of(n), cq], 0, 0)
            suffix = s if suffix is None else suffix + s
            slow[rows_of(n - 1), c] = suffix.astype(BF16)
    for h, c, ci, cw, cq in here:
        for n in range(blocks):
            r = rows_of(n)
            q, k, v, g = q_ref[r, cq], k_ref[r, ci], v_ref[r, ci], g_ref[r, ci]
            left = jnp.concatenate([bw[r, c], g], axis=1)
            right = jnp.concatenate([k, plow[r, c]], axis=0)
            qg_ref[r, c] = dot(left, right, 1, 0).astype(BF16)
            vp = dot(w_ref[r, cw], g, 0, 0)
            if n + 1 < blocks:
                left = jnp.concatenate([bw[r, c].T, v], axis=1)
                right = jnp.concatenate([q, slow[r, c]], axis=0)
                kp = dot(left, right, 1, 0)
                vp = vp + dot(k, slow[r, c], 1, 1)
            else:
                kp = dot(bw[r, c], q, 0, 0)
            kl_ref[r, c] = kp
            vl_ref[r, c] = vp
    for copy in copies:
        copy.wait()


def last_kernel(counts, before, k_ref, v_ref, s_ref, *rest):
    kls, vls, rest = rest[: len(counts)], rest[len(counts) : 2 * len(counts)], rest[2 * len(counts) :]
    old_a, old_b = rest[:2]
    heads = sum(counts)
    if before is not None:
        kg, vg, a_hbm, b_hbm, sems = rest[-5:]
        copies = flush([(old_a, a_hbm.at[:, before]), (old_b, b_hbm.at[:, before])], sems.at[0])
    else:
        a_hbm, b_hbm, kg, vg, sems = rest[-5:]
        there = slice(0, heads * HEAD_DIM)
        copies = flush([(old_a, a_hbm.at[:, there]), (old_b, b_hbm.at[:, there])], sems.at[0])
    h = 0
    for kl, vl, count in zip(kls, vls, counts):
        for i in range(count):
            c, ci = cols_of(h), cols_of(i)
            low = s_ref[h].astype(BF16)
            kg[:, c] = (kl[:, ci] + dot(v_ref[:, c], low, 1, 1)).astype(BF16)
            vg[:, c] = (vl[:, ci] + dot(k_ref[:, c], low, 1, 0)).astype(BF16)
            h += 1
            if before is None:
                to = cols_of(heads + h - 1)
                copies += flush([(kg.at[:, c], a_hbm.at[:, to]), (vg.at[:, c], b_hbm.at[:, to])], sems.at[h])
    for copy in copies:
        copy.wait()


def call(kernel, ins, outs, in_specs=None, out_specs=None, scratch=(), aliases=None, flops=0, vmem=6):
    nbytes = sum(a.size * a.dtype.itemsize for a in ins)
    return pl.pallas_call(
        kernel,
        in_specs=in_specs or [VMEM] * len(ins),
        out_specs=tuple(out_specs or [VMEM] * len(outs)),
        out_shape=tuple(jax.ShapeDtypeStruct(shape, dtype) for shape, dtype in outs),
        scratch_shapes=list(scratch),
        input_output_aliases=aliases or {},
        compiler_params=pltpu.CompilerParams(vmem_limit_bytes=vmem << 20),
        cost_estimate=pl.CostEstimate(flops=flops, bytes_accessed=nbytes, transcendentals=0),
    )(*ins)


def scan_stages(states, size, low, reverse):
    place = (lambda i: size - 1 - i) if reverse else (lambda i: i)
    perm = lambda pairs: [(place(i), place(j)) for i, j in pairs]
    outer = size // 2
    swap = [(i, i ^ 1) for i in range(size)]
    at_first = (lambda a, b: jnp.where(low, b, a)) if reverse else (lambda a, b: jnp.where(low, a, b))
    half = states.shape[0] // 2
    mine = jnp.where(low, states[:half], states[half:])
    other = jnp.where(low, states[half:], states[:half])
    got = yield other, perm(swap)
    pair = mine + got
    total = None
    if outer <= 4:
        running = pair
        for hop in range(outer - 1):
            r = yield running, perm([(2 * hop, 2 * hop + 2), (2 * hop + 1, 2 * hop + 3)])
            total = r if total is None else total + r
            running = r + pair
    else:
        total = yield pair, perm([(i, i + 2) for i in range(size - 2)])
        step = 1
        while step < outer - 1:
            r = yield total, perm([(i, i + 2 * step) for i in range(size - 2 * step)])
            total = total + r
            step *= 2
    answer = yield at_first(total + mine, total), perm(swap)
    kept = at_first(total, total + got)
    return jnp.concatenate([jnp.where(low, kept, answer), jnp.where(low, answer, kept)], axis=0)


def drive(makers, pieces, finish):
    live, behind, event = [], (), 0
    waiting = list(makers)
    while waiting or live:
        if waiting:
            scan = waiting.pop(0)()
            name, (operand, pairs) = len(makers) - len(waiting) - 1, next(scan)
        else:
            name, scan, result = live.pop(0)
            try:
                operand, pairs = scan.send(after(behind, result)[0])
            except StopIteration as stop:
                behind = finish(name, stop.value)
                continue
        live.append((name, scan, lax.ppermute(operand, "seq", pairs)))
        behind = pieces.pop(event)((operand,)) if event in pieces else ()
        event += 1
    for piece in pieces.values():
        piece(())


def after(tied, *arrays):
    return lax.optimization_barrier((*arrays, *tied))[: len(arrays)] if tied else arrays


def head_sum(a, size):
    if size & (size - 1):
        return lax.psum(a, "head")
    step = 1
    while step < size:
        a = a + lax.ppermute(a, "head", [(i, i ^ step) for i in range(size)])
        step *= 2
    return a


def body(seq_size, head_size, queries, keys, values, gain, out_grad):
    rows, width = queries.shape
    blocks, heads = rows // BLOCK, width // HEAD_DIM
    half = heads // 2
    part = half * HEAD_DIM
    low = lax.axis_index("seq") % 2 == 0
    gain = gain.reshape(1, width)
    unit = 2 * rows * HEAD_DIM * HEAD_DIM
    whole = ((rows, width), BF16)
    state = ((half, HEAD_DIM, HEAD_DIM), F32)

    ks, vs, states = [], [], []

    def piece_state(i, tied):
        k, v, t = call(
            functools.partial(load_kernel, i * half, half),
            after(tied, keys, values),
            [((rows, part), BF16), ((rows, part), BF16), state],
            in_specs=[HBM, HBM],
            scratch=[pltpu.SemaphoreType.DMA((2, half))],
            flops=unit * half,
            vmem=50,
        )
        ks.append(k)
        vs.append(v)
        states.append(t)
        return (t,)

    piece_state(0, ())

    size = min(2, half)
    weights, attended = {}, {}

    def piece_local(first, tied):
        (qt,) = after(tied, queries)
        weights[first], attended[first] = call(
            functools.partial(local_kernel, first, first % half, size, blocks),
            [qt, ks[first // half], vs[first // half]],
            [((rows, size * HEAD_DIM), BF16), ((rows, size * HEAD_DIM), F32)],
            scratch=[pltpu.VMEM((rows, HEAD_DIM), BF16)],
            flops=4 * unit * size,
        )
        return weights[first], attended[first]

    prefixes, atts, sums = [], [], []

    def make_stats(i, prefix):
        parts = [attended[first] for first in range(i * half, (i + 1) * half, size)]
        att, s = call(
            functools.partial(stats_kernel, i * half, len(parts), size, blocks),
            [*parts, queries, prefix, out_grad, gain],
            [((rows, part), F32), ((2, rows), F32)],
            flops=unit * half,
        )
        prefixes.append(prefix)
        atts.append(att)
        sums.append(s)
        return att, s

    drive(
        [lambda i=i: scan_stages(states[i], seq_size, low, False) for i in range(2)],
        {0: functools.partial(piece_state, 1), **{i + 1: functools.partial(piece_local, i * size) for i in range(heads // size)}},
        make_stats,
    )
    total = head_sum(sums[0] + sums[1], head_size)

    grads, backs, factors = [], [], []

    def piece_grad(i, tied):
        (qt,) = after(tied, queries)
        grad, back, *new = call(
            functools.partial(grad_kernel, i * half, half, blocks),
            [atts[i], qt, out_grad, gain, *(factors or [total])],
            [((rows, part), BF16), state] + ([] if factors else [((rows, BLOCK), F32)] * 2),
            flops=unit * half,
        )
        factors.extend(new)
        grads.append(grad)
        backs.append(back)
        return (back,)

    inner, made, fresh, before = {}, [], [], [None]

    def piece_back(first, count, tied):
        i = first // half
        (qt,) = after(tied, queries)
        ins = [qt, ks[i], vs[i], weights[first // size * size], grads[i], prefixes[i], atts[i], gain, factors[0], *fresh]
        own = (rows, count * HEAD_DIM)
        specs, outs, aliases = [VMEM] * len(ins), [(own, BF16)] * 2 + [(own, F32)] * 2, {}
        out_specs, scratch = [VMEM] * 4, [pltpu.VMEM(own, BF16)] * 3
        if fresh:
            aliases = {len(ins) + n: 4 + n for n in range(len(made))}
            ins, specs = ins + made, specs + [HBM] * len(made)
            outs, out_specs = outs + [whole] * 2, out_specs + [HBM] * 2
            scratch.append(pltpu.SemaphoreType.DMA((2,)))
        m, q, *others = call(
            functools.partial(back_kernel, first, count, first % half, first % size, blocks, before[0]),
            ins,
            outs,
            in_specs=specs,
            out_specs=out_specs,
            scratch=scratch,
            aliases=aliases,
            flops=9 * unit * count,
        )
        inner[first], made[:] = (count, *others[:2]), others[2:]
        fresh[:], before[0] = [m, q], slice(first * HEAD_DIM, (first + count) * HEAD_DIM)
        return tuple(others[:2])

    results = []

    def make_last(i, suffix):
        mine = [inner[first] for first in sorted(inner) if first // half == i]
        ins = [ks[i], vs[i], suffix] + [kl for _, kl, _ in mine] + [vl for _, _, vl in mine] + (results if i else fresh)
        specs, aliases = [VMEM] * len(ins), {}
        here = [((rows, part), BF16)] * 2
        if i:
            outs, out_specs, scratch = [whole] * 2, [HBM] * 2, [pltpu.VMEM(*pair) for pair in here]
        else:
            aliases = {len(ins) + n: 2 + n for n in range(len(made))}
            ins, specs = ins + made, specs + [HBM] * len(made)
            outs, out_specs, scratch = here + [whole] * 2, [VMEM] * 2 + [HBM] * 2, []
        results.clear()
        got = call(
            functools.partial(last_kernel, [count for count, _, _ in mine], None if i else before[0]),
            ins,
            outs,
            in_specs=specs,
            out_specs=out_specs,
            scratch=scratch + [pltpu.SemaphoreType.DMA((1 + half, 2))],
            aliases=aliases,
            flops=2 * unit * half,
        )
        results.extend(got[:2])
        if i == 0:
            made[:] = got[2:]
        return tuple(got)

    piece_grad(0, ())
    groups = [(0, 1), (1, 1)] + [(first, size) for first in range(2, heads, size)] if size == 2 else [(0, 1), (1, 1)]
    under = {0: [functools.partial(piece_grad, 1)]}
    for n, group in enumerate(groups):
        under.setdefault((1, 2, 3, 5)[min(n, 3)], []).append(functools.partial(piece_back, *group))

    def in_turn(works, tied):
        for work in works:
            tied = work(tied)
        return tied

    drive(
        [lambda i=i: scan_stages(backs[i], seq_size, low, True) for i in range(2)],
        {event: functools.partial(in_turn, works) for event, works in under.items()},
        make_last,
    )
    return (*made, *results)


def solution(mesh):
    placed = (P("seq", "head"), P("seq", "head"), P("seq", "head"), P("head"), P("seq", "head"))
    return jax.shard_map(
        functools.partial(body, mesh.shape["seq"], mesh.shape["head"]),
        mesh=mesh,
        in_specs=placed,
        out_specs=(P("seq", "head"),) * 4,
        check_vma=False,
    )
```

```python
import functools

import jax
import jax.numpy as jnp
from jax import lax
from jax.experimental import pallas as pl
from jax.experimental.pallas import tpu as pltpu
from jax.sharding import PartitionSpec as P

HEAD_DIM = 128
BLOCK = 128
WIDTH = 4096
epsilon = 1e-05

F32 = jnp.float32
BF16 = jnp.bfloat16
VMEM = pl.BlockSpec(memory_space=pltpu.VMEM)
HBM = pl.BlockSpec(memory_space=pltpu.HBM)


def dot(a, b, ca, cb):
    return lax.dot_general(a, b, (((ca,), (cb,)), ((), ())), preferred_element_type=F32)


def causal_mask():
    row = lax.broadcasted_iota(jnp.int32, (BLOCK, BLOCK), 0)
    col = lax.broadcasted_iota(jnp.int32, (BLOCK, BLOCK), 1)
    return col <= row


def rows_of(n):
    return slice(n * BLOCK, (n + 1) * BLOCK)


def cols_of(h):
    return slice(h * HEAD_DIM, (h + 1) * HEAD_DIM)


def places(size):
    low = 1 - lax.rem(lax.axis_index("seq"), 2)

    def columns(group, h=0, heads=1):
        chunk, own = divmod(group, 2)
        half = 2 * chunk + (1 - low if own else low)
        return pl.ds(pl.multiple_of((half * size + h) * HEAD_DIM, HEAD_DIM), heads * HEAD_DIM)

    return columns


def flush(pairs, sems):
    copies = [pltpu.make_async_copy(src, dst, sems.at[i]) for i, (src, dst) in enumerate(pairs)]
    for copy in copies:
        copy.start()
    return copies


def load_kernel(groups, size, k_hbm, v_hbm, *rest):
    count = len(groups)
    k_refs, v_refs, t_refs, sems = rest[:count], rest[count : 2 * count], rest[2 * count : 3 * count], rest[-1]
    at = places(size)
    copies = [
        flush([(k_hbm.at[:, at(g, 0, size)], k_ref), (v_hbm.at[:, at(g, 0, size)], v_ref)], sems.at[n])
        for n, (g, k_ref, v_ref) in enumerate(zip(groups, k_refs, v_refs))
    ]
    for group, k_ref, v_ref, t_ref in zip(copies, k_refs, v_refs, t_refs):
        for copy in group:
            copy.wait()
        for h in range(size):
            t_ref[h] = dot(k_ref[:, cols_of(h)], v_ref[:, cols_of(h)], 0, 0)


def local_kernel(group, size, blocks, q_ref, k_ref, v_ref, w_ref, a_ref, low):
    causal = causal_mask()
    at = places(size)
    here = [(cols_of(h), at(group, h)) for h in range(size)]
    for c, cq in here:
        for n in range(0, blocks, 2):
            r = slice(n * BLOCK, min(n + 2, blocks) * BLOCK)
            s = dot(q_ref[r, cq], k_ref[r, c], 1, 1)
            for m in range(n, min(n + 2, blocks)):
                inside = rows_of(m - n)
                w_ref[rows_of(m), c] = jnp.where(causal, s[inside, inside], 0.0).astype(BF16)
    for c, cq in here:
        prefix = None
        for n in range(blocks - 1):
            s = dot(k_ref[rows_of(n), c], v_ref[rows_of(n), c], 0, 0)
            prefix = s if prefix is None else prefix + s
            low[rows_of(n), c] = prefix.astype(BF16)
    for c, cq in here:
        a_ref[rows_of(0), c] = dot(w_ref[rows_of(0), c], v_ref[rows_of(0), c], 1, 0)
        for n in range(1, blocks):
            left = jnp.concatenate([w_ref[rows_of(n), c], q_ref[rows_of(n), cq]], axis=1)
            right = jnp.concatenate([v_ref[rows_of(n), c], low[rows_of(n - 1), c]], axis=0)
            a_ref[rows_of(n), c] = dot(left, right, 1, 0)


def stats_kernel(group, size, blocks, a_in, q_ref, p_ref, og_ref, gain_ref, a_ref, s_ref):
    at = places(size)
    low = [p_ref[h].astype(BF16) for h in range(size)]
    for n in range(blocks):
        r = rows_of(n)
        squares = dots = None
        for h in range(size):
            c, cq = cols_of(h), at(group, h)
            att = a_in[r, c] + dot(q_ref[r, cq], low[h], 1, 0)
            a_ref[r, c] = att
            scaled = gain_ref[:, cq] * og_ref[r, cq].astype(F32)
            squares = att * att if squares is None else squares + att * att
            dots = scaled * att if dots is None else dots + scaled * att
        s_ref[0:1, r] = jnp.sum(squares.T, axis=0, keepdims=True)
        s_ref[1:2, r] = jnp.sum(dots.T, axis=0, keepdims=True)


def grad_kernel(group, size, blocks, a_ref, q_ref, og_ref, gain_ref, *rest):
    if len(rest) == 5:
        s_ref, g_ref, t_ref, inv_ref, coef_ref = rest
        inverse = lax.rsqrt(s_ref[0:1, :] / WIDTH + epsilon)
        factor = inverse * inverse * inverse * s_ref[1:2, :] / WIDTH
        for n in range(blocks):
            inv_ref[rows_of(n), :] = jnp.broadcast_to(inverse[:, rows_of(n)], (BLOCK, BLOCK)).T
            coef_ref[rows_of(n), :] = jnp.broadcast_to(factor[:, rows_of(n)], (BLOCK, BLOCK)).T
    else:
        inv_ref, coef_ref, g_ref, t_ref = rest
    at = places(size)
    for h in range(size):
        c, cq = cols_of(h), at(group, h)
        scaled = gain_ref[:, cq] * og_ref[:, cq].astype(F32)
        grad = (inv_ref[...] * scaled - coef_ref[...] * a_ref[:, c]).astype(BF16)
        g_ref[:, c] = grad
        t_ref[h] = dot(q_ref[:, cq], grad, 0, 0)


def back_kernel(here, before, size, blocks, q_ref, k_ref, v_ref, w_ref, g_ref, p_ref, a_ref, gain_ref, inv_ref, *rest):
    at = places(size)
    copies = []
    if before is not None:
        old_m, old_q = rest[:2]
        m_ref, qg_ref, kl_ref, vl_ref, m_hbm, q_hbm, bw, plow, slow, sems = rest[-10:]
        there = at(*before)
        copies = flush([(old_m, m_hbm.at[:, there]), (old_q, q_hbm.at[:, there])], sems)
    else:
        m_ref, qg_ref, kl_ref, vl_ref, bw, plow, slow = rest
    causal = causal_mask()
    group, first, heads = here
    each = [(h, cols_of(h), cols_of(h + first), at(group, h + first)) for h in range(heads)]
    for h, c, ci, cq in each:
        m_ref[:, c] = (gain_ref[:, cq] * a_ref[:, ci] * inv_ref[...]).astype(BF16)
    for h, c, ci, cq in each:
        for n in range(0, blocks, 2):
            r = slice(n * BLOCK, min(n + 2, blocks) * BLOCK)
            s = dot(g_ref[r, ci], v_ref[r, ci], 1, 1)
            for m in range(n, min(n + 2, blocks)):
                inside = rows_of(m - n)
                bw[rows_of(m), c] = jnp.where(causal, s[inside, inside], 0.0).astype(BF16)
    for h, c, ci, cq in each:
        prefix = p_ref[h + first].T
        plow[rows_of(0), c] = prefix.astype(BF16)
        for n in range(blocks - 1):
            prefix = prefix + dot(v_ref[rows_of(n), ci], k_ref[rows_of(n), ci], 0, 0)
            plow[rows_of(n + 1), c] = prefix.astype(BF16)
    for h, c, ci, cq in each:
        suffix = None
        for n in reversed(range(1, blocks)):
            s = dot(g_ref[rows_of(n), ci], q_ref[rows_of(n), cq], 0, 0)
            suffix = s if suffix is None else suffix + s
            slow[rows_of(n - 1), c] = suffix.astype(BF16)
    for h, c, ci, cq in each:
        for n in range(blocks):
            r = rows_of(n)
            q, k, v, g = q_ref[r, cq], k_ref[r, ci], v_ref[r, ci], g_ref[r, ci]
            left = jnp.concatenate([bw[r, c], g], axis=1)
            right = jnp.concatenate([k, plow[r, c]], axis=0)
            qg_ref[r, c] = dot(left, right, 1, 0).astype(BF16)
            vp = dot(w_ref[r, ci], g, 0, 0)
            if n + 1 < blocks:
                left = jnp.concatenate([bw[r, c].T, v], axis=1)
                right = jnp.concatenate([q, slow[r, c]], axis=0)
                kp = dot(left, right, 1, 0)
                vp = vp + dot(k, slow[r, c], 1, 1)
            else:
                kp = dot(bw[r, c], q, 0, 0)
            kl_ref[r, c] = kp
            vl_ref[r, c] = vp
    for copy in copies:
        copy.wait()


def flush_kernel(here, size, a_ref, b_ref, *rest):
    a_hbm, b_hbm, sems = rest[-3:]
    there = places(size)(*here)
    for copy in flush([(a_ref, a_hbm.at[:, there]), (b_ref, b_hbm.at[:, there])], sems):
        copy.wait()


def last_kernel(group, counts, size, k_ref, v_ref, s_ref, *rest):
    kls, vls = rest[: len(counts)], rest[len(counts) : 2 * len(counts)]
    k_hbm, v_hbm, kg, vg, sems = rest[-5:]
    at = places(size)
    copies, h = [], 0
    for kl, vl, count in zip(kls, vls, counts):
        for i in range(count):
            c, ci, to = cols_of(h), cols_of(i), at(group, h)
            low = s_ref[h].astype(BF16)
            kg[:, c] = (kl[:, ci] + dot(v_ref[:, c], low, 1, 1)).astype(BF16)
            copies += flush([(kg.at[:, c], k_hbm.at[:, to])], sems.at[0, h : h + 1])
            vg[:, c] = (vl[:, ci] + dot(k_ref[:, c], low, 1, 0)).astype(BF16)
            copies += flush([(vg.at[:, c], v_hbm.at[:, to])], sems.at[1, h : h + 1])
            h += 1
    for copy in copies:
        copy.wait()


def call(kernel, ins, outs, in_specs=None, out_specs=None, scratch=(), aliases=None, flops=0, vmem=6):
    nbytes = sum(a.size * a.dtype.itemsize for a in ins)
    return pl.pallas_call(
        kernel,
        in_specs=in_specs or [VMEM] * len(ins),
        out_specs=tuple(out_specs or [VMEM] * len(outs)),
        out_shape=tuple(jax.ShapeDtypeStruct(shape, dtype) for shape, dtype in outs),
        scratch_shapes=list(scratch),
        input_output_aliases=aliases or {},
        compiler_params=pltpu.CompilerParams(vmem_limit_bytes=vmem << 20),
        cost_estimate=pl.CostEstimate(flops=flops, bytes_accessed=nbytes, transcendentals=0),
    )(*ins)


def scan_stages(other, mine, size, low, reverse):
    place = (lambda i: size - 1 - i) if reverse else (lambda i: i)
    perm = lambda pairs: [(place(i), place(j)) for i, j in pairs]
    at_first = (lambda a, b: jnp.where(low, b, a)) if reverse else (lambda a, b: jnp.where(low, a, b))
    outer = size // 2
    swap = [(i, i ^ 1) for i in range(size)]
    got = yield other, perm(swap), None
    mine = mine()
    pair = mine + got
    total = None
    if outer <= 4:
        running = pair
        for hop in range(outer - 1):
            r = yield running, perm([(2 * hop, 2 * hop + 2), (2 * hop + 1, 2 * hop + 3)]), None
            total = r if total is None else total + r
            running = r + pair
    else:
        total = yield pair, perm([(i, i + 2) for i in range(size - 2)]), None
        step = 1
        while step < outer - 1:
            r = yield total, perm([(i, i + 2 * step) for i in range(size - 2 * step)]), None
            total = total + r
            step *= 2
    return (yield at_first(total + mine, total), perm(swap), at_first(total, total + got))


def after(tied, *arrays):
    return lax.optimization_barrier((*arrays, *tied))[: len(arrays)] if tied else arrays


def drive(makers, pieces, early, finish):
    live, behind, event = [], (), 0
    waiting = list(makers)
    while waiting or live:
        if waiting:
            scan = waiting.pop(0)()
            name, (operand, pairs, answer) = len(makers) - len(waiting) - 1, next(scan)
        else:
            name, scan, result = live.pop(0)
            try:
                operand, pairs, answer = scan.send(after(behind, result)[0])
            except StopIteration as stop:
                behind = finish(name, stop.value)
                continue
        if answer is not None:
            early(name, answer)
        live.append((name, scan, lax.ppermute(operand, "seq", pairs)))
        behind = pieces.pop(event)((operand,)) if event in pieces else ()
        event += 1
    for piece in pieces.values():
        piece(())


def in_events(events):
    def in_turn(works, tied):
        for work in works:
            tied = work(tied)
        return tied

    return {event: functools.partial(in_turn, works) for event, works in sorted(events.items())}


def head_sum(a, size):
    if size & (size - 1):
        return lax.psum(a, "head")
    step = 1
    while step < size:
        a = a + lax.ppermute(a, "head", [(i, i ^ step) for i in range(size)])
        step *= 2
    return a


def body(seq_size, head_size, queries, keys, values, gain, out_grad):
    rows, width = queries.shape
    blocks, heads = rows // BLOCK, width // HEAD_DIM
    size = heads // 4
    low = lax.axis_index("seq") % 2 == 0
    gain = gain.reshape(1, width)
    unit = 2 * rows * HEAD_DIM * HEAD_DIM
    whole = ((rows, width), BF16)
    part = (rows, size * HEAD_DIM)
    state = ((size, HEAD_DIM, HEAD_DIM), F32)
    ks, vs, states, weights, atts, sums, prefixes, grads, backs = ({} for _ in range(9))

    outer = seq_size // 2
    last = 2 * (2 + (outer - 1 if outer <= 4 else (outer - 2).bit_length() + 1)) - 1


    def piece_load(groups, tied):
        got = call(
            functools.partial(load_kernel, groups, size),
            after(tied, keys, values),
            [(part, BF16)] * (2 * len(groups)) + [state] * len(groups),
            in_specs=[HBM, HBM],
            scratch=[pltpu.SemaphoreType.DMA((len(groups), 2))],
            flops=unit * size * len(groups),
            vmem=52 if len(groups) == 1 else 50,
        )
        count = len(groups)
        for n, g in enumerate(groups):
            ks[g], vs[g], states[g] = got[n], got[count + n], got[2 * count + n]
        return tuple(states[g] for g in groups)

    def piece_local(g, tied):
        (q,) = after(tied, queries)
        weights[g], atts[g] = call(
            functools.partial(local_kernel, g, size, blocks),
            [q, ks[g], vs[g]],
            [(part, BF16), (part, F32)],
            scratch=[pltpu.VMEM(part, BF16)],
            flops=4 * unit * size,
        )
        return weights[g], atts[g]

    def piece_stats(g, tied):
        (q,) = after(tied, queries)
        atts[g], sums[g] = call(
            functools.partial(stats_kernel, g, size, blocks),
            [atts[g], q, prefixes[g], out_grad, gain],
            [(part, F32), ((2, rows), F32)],
            flops=unit * size,
        )
        return atts[g], sums[g]

    def end_stats(i, answer):
        prefixes[2 * i] = answer
        return piece_stats(2 * i, ())

    piece_load([0], (low,))
    drive(
        [lambda i=i: scan_stages(states[2 * i], lambda: states[2 * i + 1], seq_size, low, False) for i in range(2)],
        in_events({
            0: [functools.partial(piece_load, [1, 2, 3])],
            2: [functools.partial(piece_local, 0)],
            3: [functools.partial(piece_local, 1)],
            4: [functools.partial(piece_local, 2)],
            5: [functools.partial(piece_local, 3)],
            last: [functools.partial(piece_stats, 1), functools.partial(piece_stats, 3)],
        }),
        lambda i, answer: prefixes.update({2 * i + 1: answer}),
        end_stats,
    )
    total = head_sum(sum(sums[g] for g in range(1, 4)) + sums[0], head_size)

    factors, inner, made, fresh, before, suffixes, results = [], {}, [], [], [None], {}, []

    def piece_grad(g, tied):
        (q,) = after(tied, queries)
        grads[g], backs[g], *new = call(
            functools.partial(grad_kernel, g, size, blocks),
            [atts[g], q, out_grad, gain, *(factors or [total])],
            [(part, BF16), state] + ([] if factors else [((rows, BLOCK), F32)] * 2),
            flops=unit * size,
        )
        factors.extend(new)
        return (backs[g],)

    def piece_back(g, first, count, tied):
        (q,) = after(tied, queries)
        ins = [q, ks[g], vs[g], weights[g], grads[g], prefixes[g], atts[g], gain, factors[0], *fresh]
        own = (rows, count * HEAD_DIM)
        specs, outs, aliases = [VMEM] * len(ins), [(own, BF16)] * 2 + [(own, F32)] * 2, {}
        out_specs, scratch = [VMEM] * 4, [pltpu.VMEM(own, BF16)] * 3
        if fresh:
            aliases = {len(ins) + n: 4 + n for n in range(len(made))}
            ins, specs = ins + made, specs + [HBM] * len(made)
            outs, out_specs = outs + [whole] * 2, out_specs + [HBM] * 2
            scratch.append(pltpu.SemaphoreType.DMA((2,)))
        m, q, *others = call(
            functools.partial(back_kernel, (g, first, count), before[0], size, blocks),
            ins,
            outs,
            in_specs=specs,
            out_specs=out_specs,
            scratch=scratch,
            aliases=aliases,
            flops=9 * unit * count,
        )
        inner[g, first], made[:] = (count, *others[:2]), others[2:]
        fresh[:], before[0] = [m, q], (g, first, count)
        return tuple(others[:2])

    def piece_flush(tied):
        ins, into = [*after(tied, fresh[0]), fresh[1]], list(made)
        made[:] = call(
            functools.partial(flush_kernel, before[0], size),
            ins + into,
            [whole] * 2,
            in_specs=[VMEM] * 2 + [HBM] * len(into),
            out_specs=[HBM] * 2,
            scratch=[pltpu.SemaphoreType.DMA((2,))],
            aliases={2 + n: n for n in range(len(into))},
        )
        return tuple(made)

    def piece_last(g, tied):
        mine = [inner[key] for key in sorted(inner) if key[0] == g]
        ins = [*after(tied, ks[g]), vs[g], suffixes[g]] + [kl for _, kl, _ in mine] + [vl for _, _, vl in mine]
        results[:] = call(
            functools.partial(last_kernel, g, [count for count, _, _ in mine], size),
            ins + results,
            [whole] * 2,
            in_specs=[VMEM] * len(ins) + [HBM] * len(results),
            out_specs=[HBM] * 2,
            scratch=[pltpu.VMEM(part, BF16)] * 2 + [pltpu.SemaphoreType.DMA((2, size))],
            aliases={len(ins) + n: n for n in range(len(results))},
            flops=2 * unit * size,
        )
        return tuple(results)

    def end_last(i, answer):
        suffixes[2 * i] = answer
        return piece_last(2 * i, ())

    piece_grad(0, ())
    drive(
        [lambda i=i: scan_stages(backs[2 * i], lambda: backs[2 * i + 1], seq_size, low, True) for i in range(2)],
        in_events({
            0: [functools.partial(piece_grad, 2)],
            1: [functools.partial(piece_grad, 1), functools.partial(piece_grad, 3)],
            2: [functools.partial(piece_back, 0, 0, size)],
            3: [functools.partial(piece_back, 1, 0, size)],
            5: [functools.partial(piece_back, 2, 0, size), functools.partial(piece_back, 3, 0, size), piece_flush],
            last: [functools.partial(piece_last, 1), functools.partial(piece_last, 3)],
        }),
        lambda i, answer: suffixes.update({2 * i + 1: answer}),
        end_last,
    )
    return (*made, *results)


def solution(mesh):
    placed = (P("seq", "head"), P("seq", "head"), P("seq", "head"), P("head"), P("seq", "head"))
    return jax.shard_map(
        functools.partial(body, mesh.shape["seq"], mesh.shape["head"]),
        mesh=mesh,
        in_specs=placed,
        out_specs=(P("seq", "head"),) * 4,
        check_vma=False,
    )
```

```python
import functools

import jax
import jax.numpy as jnp
from jax import lax
from jax.experimental import pallas as pl
from jax.experimental.pallas import tpu as pltpu
from jax.sharding import PartitionSpec as P

HEAD_DIM = 128
BLOCK = 128
WIDTH = 4096
epsilon = 1e-05

F32 = jnp.float32
BF16 = jnp.bfloat16
VMEM = pl.BlockSpec(memory_space=pltpu.VMEM)
HBM = pl.BlockSpec(memory_space=pltpu.HBM)


def dot(a, b, ca, cb):
    return lax.dot_general(a, b, (((ca,), (cb,)), ((), ())), preferred_element_type=F32)


def causal_mask():
    row = lax.broadcasted_iota(jnp.int32, (BLOCK, BLOCK), 0)
    col = lax.broadcasted_iota(jnp.int32, (BLOCK, BLOCK), 1)
    return col <= row


def rows_of(n):
    return slice(n * BLOCK, (n + 1) * BLOCK)


def cols_of(h):
    return slice(h * HEAD_DIM, (h + 1) * HEAD_DIM)


def places(size):
    low = 1 - lax.rem(lax.axis_index("seq"), 2)

    def columns(group, h=0, heads=1):
        chunk, own = divmod(group, 2)
        half = 2 * chunk + (1 - low if own else low)
        return pl.ds(pl.multiple_of((half * size + h) * HEAD_DIM, HEAD_DIM), heads * HEAD_DIM)

    return columns


def flush(pairs, sems):
    copies = [pltpu.make_async_copy(src, dst, sems.at[i]) for i, (src, dst) in enumerate(pairs)]
    for copy in copies:
        copy.start()
    return copies


def load_kernel(groups, size, k_hbm, v_hbm, *rest):
    count = len(groups)
    k_refs, v_refs, t_refs, sems = rest[:count], rest[count : 2 * count], rest[2 * count : 3 * count], rest[-1]
    at = places(size)
    copies = [
        flush([(k_hbm.at[:, at(g, 0, size)], k_ref), (v_hbm.at[:, at(g, 0, size)], v_ref)], sems.at[n])
        for n, (g, k_ref, v_ref) in enumerate(zip(groups, k_refs, v_refs))
    ]
    for group, k_ref, v_ref, t_ref in zip(copies, k_refs, v_refs, t_refs):
        for copy in group:
            copy.wait()
        for h in range(size):
            t_ref[h] = dot(k_ref[:, cols_of(h)], v_ref[:, cols_of(h)], 0, 0)


def local_kernel(group, size, blocks, q_ref, k_ref, v_ref, w_ref, a_ref, low):
    causal = causal_mask()
    at = places(size)
    here = [(cols_of(h), at(group, h)) for h in range(size)]
    for c, cq in here:
        for n in range(0, blocks, 2):
            r = slice(n * BLOCK, min(n + 2, blocks) * BLOCK)
            s = dot(q_ref[r, cq], k_ref[r, c], 1, 1)
            for m in range(n, min(n + 2, blocks)):
                inside = rows_of(m - n)
                w_ref[rows_of(m), c] = jnp.where(causal, s[inside, inside], 0.0).astype(BF16)
    for c, cq in here:
        prefix = None
        for n in range(blocks - 1):
            s = dot(k_ref[rows_of(n), c], v_ref[rows_of(n), c], 0, 0)
            prefix = s if prefix is None else prefix + s
            low[rows_of(n), c] = prefix.astype(BF16)
    for c, cq in here:
        a_ref[rows_of(0), c] = dot(w_ref[rows_of(0), c], v_ref[rows_of(0), c], 1, 0)
        for n in range(1, blocks):
            left = jnp.concatenate([w_ref[rows_of(n), c], q_ref[rows_of(n), cq]], axis=1)
            right = jnp.concatenate([v_ref[rows_of(n), c], low[rows_of(n - 1), c]], axis=0)
            a_ref[rows_of(n), c] = dot(left, right, 1, 0)


def stats_kernel(group, size, blocks, a_in, q_ref, p_ref, og_ref, gain_ref, a_ref, s_ref):
    at = places(size)
    low = [p_ref[h].astype(BF16) for h in range(size)]
    for n in range(blocks):
        r = rows_of(n)
        squares = dots = None
        for h in range(size):
            c, cq = cols_of(h), at(group, h)
            att = a_in[r, c] + dot(q_ref[r, cq], low[h], 1, 0)
            a_ref[r, c] = att
            scaled = gain_ref[:, cq] * og_ref[r, cq].astype(F32)
            squares = att * att if squares is None else squares + att * att
            dots = scaled * att if dots is None else dots + scaled * att
        s_ref[0:1, r] = jnp.sum(squares.T, axis=0, keepdims=True)
        s_ref[1:2, r] = jnp.sum(dots.T, axis=0, keepdims=True)


def grad_kernel(group, size, blocks, a_ref, q_ref, og_ref, gain_ref, *rest):
    if len(rest) == 5:
        s_ref, g_ref, t_ref, inv_ref, coef_ref = rest
        inverse = lax.rsqrt(s_ref[0:1, :] / WIDTH + epsilon)
        factor = inverse * inverse * inverse * s_ref[1:2, :] / WIDTH
        for n in range(blocks):
            inv_ref[rows_of(n), :] = jnp.broadcast_to(inverse[:, rows_of(n)], (BLOCK, BLOCK)).T
            coef_ref[rows_of(n), :] = jnp.broadcast_to(factor[:, rows_of(n)], (BLOCK, BLOCK)).T
    else:
        inv_ref, coef_ref, g_ref, t_ref = rest
    at = places(size)
    for h in range(size):
        c, cq = cols_of(h), at(group, h)
        scaled = gain_ref[:, cq] * og_ref[:, cq].astype(F32)
        grad = (inv_ref[...] * scaled - coef_ref[...] * a_ref[:, c]).astype(BF16)
        g_ref[:, c] = grad
        t_ref[h] = dot(q_ref[:, cq], grad, 0, 0)


def back_kernel(here, before, size, blocks, q_ref, k_ref, v_ref, w_ref, g_ref, p_ref, a_ref, gain_ref, inv_ref, *rest):
    at = places(size)
    copies = []
    if before:
        m_ref, qg_ref, kl_ref, vl_ref, m_hbm, q_hbm, bw, plow, slow, sems = rest[-10:]
        for n, where in enumerate(before):
            there = at(*where)
            copies += flush([(rest[2 * n], m_hbm.at[:, there]), (rest[2 * n + 1], q_hbm.at[:, there])], sems.at[n])
    else:
        m_ref, qg_ref, kl_ref, vl_ref, bw, plow, slow = rest
    causal = causal_mask()
    group, first, heads = here
    each = [(h, cols_of(h), cols_of(h + first), at(group, h + first)) for h in range(heads)]
    for h, c, ci, cq in each:
        m_ref[:, c] = (gain_ref[:, cq] * a_ref[:, ci] * inv_ref[...]).astype(BF16)
    for h, c, ci, cq in each:
        for n in range(0, blocks, 2):
            r = slice(n * BLOCK, min(n + 2, blocks) * BLOCK)
            s = dot(g_ref[r, ci], v_ref[r, ci], 1, 1)
            for m in range(n, min(n + 2, blocks)):
                inside = rows_of(m - n)
                bw[rows_of(m), c] = jnp.where(causal, s[inside, inside], 0.0).astype(BF16)
    for h, c, ci, cq in each:
        prefix = p_ref[h + first].T
        plow[rows_of(0), c] = prefix.astype(BF16)
        for n in range(blocks - 1):
            prefix = prefix + dot(v_ref[rows_of(n), ci], k_ref[rows_of(n), ci], 0, 0)
            plow[rows_of(n + 1), c] = prefix.astype(BF16)
    for h, c, ci, cq in each:
        suffix = None
        for n in reversed(range(1, blocks)):
            s = dot(g_ref[rows_of(n), ci], q_ref[rows_of(n), cq], 0, 0)
            suffix = s if suffix is None else suffix + s
            slow[rows_of(n - 1), c] = suffix.astype(BF16)
    for h, c, ci, cq in each:
        for n in range(blocks):
            r = rows_of(n)
            q, k, v, g = q_ref[r, cq], k_ref[r, ci], v_ref[r, ci], g_ref[r, ci]
            left = jnp.concatenate([bw[r, c], g], axis=1)
            right = jnp.concatenate([k, plow[r, c]], axis=0)
            qg_ref[r, c] = dot(left, right, 1, 0).astype(BF16)
            vp = dot(w_ref[r, ci], g, 0, 0)
            if n + 1 < blocks:
                left = jnp.concatenate([bw[r, c].T, v], axis=1)
                right = jnp.concatenate([q, slow[r, c]], axis=0)
                kp = dot(left, right, 1, 0)
                vp = vp + dot(k, slow[r, c], 1, 1)
            else:
                kp = dot(bw[r, c], q, 0, 0)
            kl_ref[r, c] = kp
            vl_ref[r, c] = vp
    for copy in copies:
        copy.wait()


def flush_kernel(here, size, a_ref, b_ref, *rest):
    a_hbm, b_hbm, sems = rest[-3:]
    there = places(size)(*here)
    for copy in flush([(a_ref, a_hbm.at[:, there]), (b_ref, b_hbm.at[:, there])], sems):
        copy.wait()


def last_kernel(group, counts, size, k_ref, v_ref, s_ref, *rest):
    kls, vls = rest[: len(counts)], rest[len(counts) : 2 * len(counts)]
    k_hbm, v_hbm, kg, vg, sems = rest[-5:]
    at = places(size)
    copies, h = [], 0
    for kl, vl, count in zip(kls, vls, counts):
        for i in range(count):
            c, ci, to = cols_of(h), cols_of(i), at(group, h)
            low = s_ref[h].astype(BF16)
            kg[:, c] = (kl[:, ci] + dot(v_ref[:, c], low, 1, 1)).astype(BF16)
            copies += flush([(kg.at[:, c], k_hbm.at[:, to])], sems.at[0, h : h + 1])
            vg[:, c] = (vl[:, ci] + dot(k_ref[:, c], low, 1, 0)).astype(BF16)
            copies += flush([(vg.at[:, c], v_hbm.at[:, to])], sems.at[1, h : h + 1])
            h += 1
    for copy in copies:
        copy.wait()


def call(kernel, ins, outs, in_specs=None, out_specs=None, scratch=(), aliases=None, flops=0, vmem=6):
    nbytes = sum(a.size * a.dtype.itemsize for a in ins)
    return pl.pallas_call(
        kernel,
        in_specs=in_specs or [VMEM] * len(ins),
        out_specs=tuple(out_specs or [VMEM] * len(outs)),
        out_shape=tuple(jax.ShapeDtypeStruct(shape, dtype) for shape, dtype in outs),
        scratch_shapes=list(scratch),
        input_output_aliases=aliases or {},
        compiler_params=pltpu.CompilerParams(vmem_limit_bytes=vmem << 20),
        cost_estimate=pl.CostEstimate(flops=flops, bytes_accessed=nbytes, transcendentals=0),
    )(*ins)


def scan_stages(other, mine, size, low, reverse):
    place = (lambda i: size - 1 - i) if reverse else (lambda i: i)
    perm = lambda pairs: [(place(i), place(j)) for i, j in pairs]
    at_first = (lambda a, b: jnp.where(low, b, a)) if reverse else (lambda a, b: jnp.where(low, a, b))
    outer = size // 2
    swap = [(i, i ^ 1) for i in range(size)]
    got = yield other, perm(swap), None
    mine = mine()
    pair = mine + got
    total = None
    if outer <= 4:
        running = pair
        for hop in range(outer - 1):
            r = yield running, perm([(2 * hop, 2 * hop + 2), (2 * hop + 1, 2 * hop + 3)]), None
            total = r if total is None else total + r
            running = r + pair
    else:
        total = yield pair, perm([(i, i + 2) for i in range(size - 2)]), None
        step = 1
        while step < outer - 1:
            r = yield total, perm([(i, i + 2 * step) for i in range(size - 2 * step)]), None
            total = total + r
            step *= 2
    return (yield at_first(total + mine, total), perm(swap), at_first(total, total + got))


def after(tied, *arrays):
    return lax.optimization_barrier((*arrays, *tied))[: len(arrays)] if tied else arrays


def drive(makers, pieces, early, finish):
    live, behind, event = [], (), 0
    waiting = list(makers)
    while waiting or live:
        if waiting:
            scan = waiting.pop(0)()
            name, (operand, pairs, answer) = len(makers) - len(waiting) - 1, next(scan)
        else:
            name, scan, result = live.pop(0)
            try:
                operand, pairs, answer = scan.send(after(behind, result)[0])
            except StopIteration as stop:
                behind = finish(name, stop.value)
                continue
        if answer is not None:
            early(name, answer)
        live.append((name, scan, lax.ppermute(operand, "seq", pairs)))
        behind = pieces.pop(event)((operand,)) if event in pieces else ()
        event += 1
    for piece in pieces.values():
        piece(())


def in_events(events):
    def in_turn(works, tied):
        for work in works:
            tied = work(tied)
        return tied

    return {event: functools.partial(in_turn, works) for event, works in sorted(events.items())}


def head_sum(a, size):
    if size & (size - 1):
        return lax.psum(a, "head")
    step = 1
    while step < size:
        a = a + lax.ppermute(a, "head", [(i, i ^ step) for i in range(size)])
        step *= 2
    return a


def body(seq_size, head_size, queries, keys, values, gain, out_grad):
    rows, width = queries.shape
    blocks, heads = rows // BLOCK, width // HEAD_DIM
    size = heads // 4
    low = lax.axis_index("seq") % 2 == 0
    gain = gain.reshape(1, width)
    unit = 2 * rows * HEAD_DIM * HEAD_DIM
    whole = ((rows, width), BF16)
    part = (rows, size * HEAD_DIM)
    state = ((size, HEAD_DIM, HEAD_DIM), F32)
    ks, vs, states, weights, atts, sums, prefixes, grads, backs = ({} for _ in range(9))

    outer = seq_size // 2
    last = 2 * (2 + (outer - 1 if outer <= 4 else (outer - 2).bit_length() + 1)) - 1


    def piece_load(groups, tied):
        got = call(
            functools.partial(load_kernel, groups, size),
            after(tied, keys, values),
            [(part, BF16)] * (2 * len(groups)) + [state] * len(groups),
            in_specs=[HBM, HBM],
            scratch=[pltpu.SemaphoreType.DMA((len(groups), 2))],
            flops=unit * size * len(groups),
            vmem=52 if len(groups) == 1 else 50,
        )
        count = len(groups)
        for n, g in enumerate(groups):
            ks[g], vs[g], states[g] = got[n], got[count + n], got[2 * count + n]
        return tuple(states[g] for g in groups)

    def piece_local(g, tied):
        (q,) = after(tied, queries)
        weights[g], atts[g] = call(
            functools.partial(local_kernel, g, size, blocks),
            [q, ks[g], vs[g]],
            [(part, BF16), (part, F32)],
            scratch=[pltpu.VMEM(part, BF16)],
            flops=4 * unit * size,
        )
        return weights[g], atts[g]

    def piece_stats(g, tied):
        (q,) = after(tied, queries)
        atts[g], sums[g] = call(
            functools.partial(stats_kernel, g, size, blocks),
            [atts[g], q, prefixes[g], out_grad, gain],
            [(part, F32), ((2, rows), F32)],
            flops=unit * size,
        )
        return atts[g], sums[g]

    def end_stats(i, answer):
        prefixes[2 * i] = answer
        return piece_stats(2 * i, ())

    piece_load([0], (low,))
    drive(
        [lambda i=i: scan_stages(states[2 * i], lambda: states[2 * i + 1], seq_size, low, False) for i in range(2)],
        in_events({
            0: [functools.partial(piece_load, [1, 2, 3])],
            3: [functools.partial(piece_local, 0), functools.partial(piece_local, 1)],
            5: [functools.partial(piece_local, 2), functools.partial(piece_local, 3)],
            last: [functools.partial(piece_stats, 1), functools.partial(piece_stats, 3)],
        }),
        lambda i, answer: prefixes.update({2 * i + 1: answer}),
        end_stats,
    )
    total = head_sum(sum(sums[g] for g in range(1, 4)) + sums[0], head_size)

    factors, inner, made, fresh, suffixes, results = [], {}, [], [], {}, []

    def piece_grad(g, tied):
        (q,) = after(tied, queries)
        grads[g], backs[g], *new = call(
            functools.partial(grad_kernel, g, size, blocks),
            [atts[g], q, out_grad, gain, *(factors or [total])],
            [(part, BF16), state] + ([] if factors else [((rows, BLOCK), F32)] * 2),
            flops=unit * size,
        )
        factors.extend(new)
        return (backs[g],)

    def piece_back(g, first, count, out, tied):
        (q,) = after(tied, queries)
        old = list(fresh) if out else []
        ins = [q, ks[g], vs[g], weights[g], grads[g], prefixes[g], atts[g], gain, factors[0]]
        ins += [a for _, *pair in old for a in pair]
        own = (rows, count * HEAD_DIM)
        specs, outs, aliases = [VMEM] * len(ins), [(own, BF16)] * 2 + [(own, F32)] * 2, {}
        out_specs, scratch = [VMEM] * 4, [pltpu.VMEM(own, BF16)] * 3
        if old:
            aliases = {len(ins) + n: 4 + n for n in range(len(made))}
            ins, specs = ins + made, specs + [HBM] * len(made)
            outs, out_specs = outs + [whole] * 2, out_specs + [HBM] * 2
            scratch.append(pltpu.SemaphoreType.DMA((len(old), 2)))
        m, q, *others = call(
            functools.partial(back_kernel, (g, first, count), [where for where, _, _ in old], size, blocks),
            ins,
            outs,
            in_specs=specs,
            out_specs=out_specs,
            scratch=scratch,
            aliases=aliases,
            flops=9 * unit * count,
        )
        inner[g, first] = (count, *others[:2])
        if old:
            made[:] = others[2:]
            fresh.clear()
        fresh.append(((g, first, count), m, q))
        return tuple(others[:2])

    def piece_flush(tied):
        ((where, m, q),) = fresh
        ins, into = [*after(tied, m), q], list(made)
        made[:] = call(
            functools.partial(flush_kernel, where, size),
            ins + into,
            [whole] * 2,
            in_specs=[VMEM] * 2 + [HBM] * len(into),
            out_specs=[HBM] * 2,
            scratch=[pltpu.SemaphoreType.DMA((2,))],
            aliases={2 + n: n for n in range(len(into))},
        )
        return tuple(made)

    def piece_last(g, tied):
        mine = [inner[key] for key in sorted(inner) if key[0] == g]
        ins = [*after(tied, ks[g]), vs[g], suffixes[g]] + [kl for _, kl, _ in mine] + [vl for _, _, vl in mine]
        results[:] = call(
            functools.partial(last_kernel, g, [count for count, _, _ in mine], size),
            ins + results,
            [whole] * 2,
            in_specs=[VMEM] * len(ins) + [HBM] * len(results),
            out_specs=[HBM] * 2,
            scratch=[pltpu.VMEM(part, BF16)] * 2 + [pltpu.SemaphoreType.DMA((2, size))],
            aliases={len(ins) + n: n for n in range(len(results))},
            flops=2 * unit * size,
        )
        return tuple(results)

    def end_last(i, answer):
        suffixes[2 * i] = answer
        return piece_last(2 * i, ())

    piece_grad(0, ())
    drive(
        [lambda i=i: scan_stages(backs[2 * i], lambda: backs[2 * i + 1], seq_size, low, True) for i in range(2)],
        in_events({
            0: [functools.partial(piece_grad, 2), functools.partial(piece_grad, 1)],
            1: [functools.partial(piece_grad, 3)],
            3: [functools.partial(piece_back, 0, 0, size, False), functools.partial(piece_back, 1, 0, size, False)],
            5: [functools.partial(piece_back, 2, 0, size, True), functools.partial(piece_back, 3, 0, size, True), piece_flush],
            last: [functools.partial(piece_last, 1), functools.partial(piece_last, 3)],
        }),
        lambda i, answer: suffixes.update({2 * i + 1: answer}),
        end_last,
    )
    return (*made, *results)


def solution(mesh):
    placed = (P("seq", "head"), P("seq", "head"), P("seq", "head"), P("head"), P("seq", "head"))
    return jax.shard_map(
        functools.partial(body, mesh.shape["seq"], mesh.shape["head"]),
        mesh=mesh,
        in_specs=placed,
        out_specs=(P("seq", "head"),) * 4,
        check_vma=False,
    )
```

```python
import functools

import jax
import jax.numpy as jnp
from jax import lax
from jax.experimental import pallas as pl
from jax.experimental.pallas import tpu as pltpu
from jax.sharding import PartitionSpec as P

HEAD_DIM = 128
BLOCK = 128
WIDTH = 4096
epsilon = 1e-05

F32 = jnp.float32
BF16 = jnp.bfloat16
VMEM = pl.BlockSpec(memory_space=pltpu.VMEM)
HBM = pl.BlockSpec(memory_space=pltpu.HBM)


def dot(a, b, ca, cb):
    return lax.dot_general(a, b, (((ca,), (cb,)), ((), ())), preferred_element_type=F32)


def causal_mask():
    row = lax.broadcasted_iota(jnp.int32, (BLOCK, BLOCK), 0)
    col = lax.broadcasted_iota(jnp.int32, (BLOCK, BLOCK), 1)
    return col <= row


def rows_of(n):
    return slice(n * BLOCK, (n + 1) * BLOCK)


def cols_of(h):
    return slice(h * HEAD_DIM, (h + 1) * HEAD_DIM)


def places(size):
    low = 1 - lax.rem(lax.axis_index("seq"), 2)

    def columns(group, h=0, heads=1):
        chunk, own = divmod(group, 2)
        half = 2 * chunk + (1 - low if own else low)
        return pl.ds(pl.multiple_of((half * size + h) * HEAD_DIM, HEAD_DIM), heads * HEAD_DIM)

    return columns


def flush(pairs, sems):
    copies = [pltpu.make_async_copy(src, dst, sems.at[i]) for i, (src, dst) in enumerate(pairs)]
    for copy in copies:
        copy.start()
    return copies


def load_kernel(groups, size, k_hbm, v_hbm, *rest):
    count = len(groups)
    k_refs, v_refs, t_refs, sems = rest[:count], rest[count : 2 * count], rest[2 * count : 3 * count], rest[-1]
    at = places(size)
    copies = [
        flush([(k_hbm.at[:, at(g, 0, size)], k_ref), (v_hbm.at[:, at(g, 0, size)], v_ref)], sems.at[n])
        for n, (g, k_ref, v_ref) in enumerate(zip(groups, k_refs, v_refs))
    ]
    for group, k_ref, v_ref, t_ref in zip(copies, k_refs, v_refs, t_refs):
        for copy in group:
            copy.wait()
        for h in range(size):
            t_ref[h] = dot(k_ref[:, cols_of(h)], v_ref[:, cols_of(h)], 0, 0)


def local_kernel(group, size, blocks, q_ref, k_ref, v_ref, w_ref, a_ref, low):
    causal = causal_mask()
    at = places(size)
    here = [(cols_of(h), at(group, h)) for h in range(size)]
    for c, cq in here:
        for n in range(0, blocks, 2):
            r = slice(n * BLOCK, min(n + 2, blocks) * BLOCK)
            s = dot(q_ref[r, cq], k_ref[r, c], 1, 1)
            for m in range(n, min(n + 2, blocks)):
                inside = rows_of(m - n)
                w_ref[rows_of(m), c] = jnp.where(causal, s[inside, inside], 0.0).astype(BF16)
    for c, cq in here:
        prefix = None
        for n in range(blocks - 1):
            s = dot(k_ref[rows_of(n), c], v_ref[rows_of(n), c], 0, 0)
            prefix = s if prefix is None else prefix + s
            low[rows_of(n), c] = prefix.astype(BF16)
    for c, cq in here:
        a_ref[rows_of(0), c] = dot(w_ref[rows_of(0), c], v_ref[rows_of(0), c], 1, 0)
        for n in range(1, blocks):
            left = jnp.concatenate([w_ref[rows_of(n), c], q_ref[rows_of(n), cq]], axis=1)
            right = jnp.concatenate([v_ref[rows_of(n), c], low[rows_of(n - 1), c]], axis=0)
            a_ref[rows_of(n), c] = dot(left, right, 1, 0)


def stats_kernel(group, size, blocks, a_in, q_ref, p_ref, og_ref, gain_ref, a_ref, s_ref):
    at = places(size)
    low = [p_ref[h].astype(BF16) for h in range(size)]
    for n in range(blocks):
        r = rows_of(n)
        squares = dots = None
        for h in range(size):
            c, cq = cols_of(h), at(group, h)
            att = a_in[r, c] + dot(q_ref[r, cq], low[h], 1, 0)
            a_ref[r, c] = att
            scaled = gain_ref[:, cq] * og_ref[r, cq].astype(F32)
            squares = att * att if squares is None else squares + att * att
            dots = scaled * att if dots is None else dots + scaled * att
        s_ref[0:1, r] = jnp.sum(squares.T, axis=0, keepdims=True)
        s_ref[1:2, r] = jnp.sum(dots.T, axis=0, keepdims=True)


def grad_kernel(group, size, blocks, a_ref, q_ref, og_ref, gain_ref, *rest):
    if len(rest) == 5:
        s_ref, g_ref, t_ref, inv_ref, coef_ref = rest
        inverse = lax.rsqrt(s_ref[0:1, :] / WIDTH + epsilon)
        factor = inverse * inverse * inverse * s_ref[1:2, :] / WIDTH
        for n in range(blocks):
            inv_ref[rows_of(n), :] = jnp.broadcast_to(inverse[:, rows_of(n)], (BLOCK, BLOCK)).T
            coef_ref[rows_of(n), :] = jnp.broadcast_to(factor[:, rows_of(n)], (BLOCK, BLOCK)).T
    else:
        inv_ref, coef_ref, g_ref, t_ref = rest
    at = places(size)
    for h in range(size):
        c, cq = cols_of(h), at(group, h)
        scaled = gain_ref[:, cq] * og_ref[:, cq].astype(F32)
        grad = (inv_ref[...] * scaled - coef_ref[...] * a_ref[:, c]).astype(BF16)
        g_ref[:, c] = grad
        t_ref[h] = dot(q_ref[:, cq], grad, 0, 0)


def back_kernel(here, before, size, blocks, q_ref, k_ref, v_ref, w_ref, g_ref, p_ref, a_ref, gain_ref, inv_ref, *rest):
    at = places(size)
    copies = []
    if before:
        m_ref, qg_ref, kl_ref, vl_ref, m_hbm, q_hbm, bw, plow, slow, sems = rest[-10:]
        for n, where in enumerate(before):
            there = at(*where)
            copies += flush([(rest[2 * n], m_hbm.at[:, there]), (rest[2 * n + 1], q_hbm.at[:, there])], sems.at[n])
    else:
        m_ref, qg_ref, kl_ref, vl_ref, bw, plow, slow = rest
    causal = causal_mask()
    group, first, heads = here
    each = [(h, cols_of(h), cols_of(h + first), at(group, h + first)) for h in range(heads)]
    for h, c, ci, cq in each:
        m_ref[:, c] = (gain_ref[:, cq] * a_ref[:, ci] * inv_ref[...]).astype(BF16)
    for h, c, ci, cq in each:
        for n in range(0, blocks, 2):
            r = slice(n * BLOCK, min(n + 2, blocks) * BLOCK)
            s = dot(g_ref[r, ci], v_ref[r, ci], 1, 1)
            for m in range(n, min(n + 2, blocks)):
                inside = rows_of(m - n)
                bw[rows_of(m), c] = jnp.where(causal, s[inside, inside], 0.0).astype(BF16)
    for h, c, ci, cq in each:
        prefix = p_ref[h + first].T
        plow[rows_of(0), c] = prefix.astype(BF16)
        for n in range(blocks - 1):
            prefix = prefix + dot(v_ref[rows_of(n), ci], k_ref[rows_of(n), ci], 0, 0)
            plow[rows_of(n + 1), c] = prefix.astype(BF16)
    for h, c, ci, cq in each:
        suffix = None
        for n in reversed(range(1, blocks)):
            s = dot(g_ref[rows_of(n), ci], q_ref[rows_of(n), cq], 0, 0)
            suffix = s if suffix is None else suffix + s
            slow[rows_of(n - 1), c] = suffix.astype(BF16)
    for h, c, ci, cq in each:
        for n in range(blocks):
            r = rows_of(n)
            q, k, v, g = q_ref[r, cq], k_ref[r, ci], v_ref[r, ci], g_ref[r, ci]
            left = jnp.concatenate([bw[r, c], g], axis=1)
            right = jnp.concatenate([k, plow[r, c]], axis=0)
            qg_ref[r, c] = dot(left, right, 1, 0).astype(BF16)
            vp = dot(w_ref[r, ci], g, 0, 0)
            if n + 1 < blocks:
                left = jnp.concatenate([bw[r, c].T, v], axis=1)
                right = jnp.concatenate([q, slow[r, c]], axis=0)
                kp = dot(left, right, 1, 0)
                vp = vp + dot(k, slow[r, c], 1, 1)
            else:
                kp = dot(bw[r, c], q, 0, 0)
            kl_ref[r, c] = kp
            vl_ref[r, c] = vp
    for copy in copies:
        copy.wait()


def flush_kernel(here, size, a_ref, b_ref, *rest):
    a_hbm, b_hbm, sems = rest[-3:]
    there = places(size)(*here)
    for copy in flush([(a_ref, a_hbm.at[:, there]), (b_ref, b_hbm.at[:, there])], sems):
        copy.wait()


def last_kernel(group, counts, size, k_ref, v_ref, s_ref, *rest):
    kls, vls = rest[: len(counts)], rest[len(counts) : 2 * len(counts)]
    k_hbm, v_hbm, kg, vg, sems = rest[-5:]
    at = places(size)
    copies, h = [], 0
    for kl, vl, count in zip(kls, vls, counts):
        for i in range(count):
            c, ci, to = cols_of(h), cols_of(i), at(group, h)
            low = s_ref[h].astype(BF16)
            kg[:, c] = (kl[:, ci] + dot(v_ref[:, c], low, 1, 1)).astype(BF16)
            copies += flush([(kg.at[:, c], k_hbm.at[:, to])], sems.at[0, h : h + 1])
            vg[:, c] = (vl[:, ci] + dot(k_ref[:, c], low, 1, 0)).astype(BF16)
            copies += flush([(vg.at[:, c], v_hbm.at[:, to])], sems.at[1, h : h + 1])
            h += 1
    for copy in copies:
        copy.wait()


def call(kernel, ins, outs, in_specs=None, out_specs=None, scratch=(), aliases=None, flops=0, vmem=6):
    nbytes = sum(a.size * a.dtype.itemsize for a in ins)
    return pl.pallas_call(
        kernel,
        in_specs=in_specs or [VMEM] * len(ins),
        out_specs=tuple(out_specs or [VMEM] * len(outs)),
        out_shape=tuple(jax.ShapeDtypeStruct(shape, dtype) for shape, dtype in outs),
        scratch_shapes=list(scratch),
        input_output_aliases=aliases or {},
        compiler_params=pltpu.CompilerParams(vmem_limit_bytes=vmem << 20),
        cost_estimate=pl.CostEstimate(flops=flops, bytes_accessed=nbytes, transcendentals=0),
    )(*ins)


def scan_stages(other, mine, size, low, reverse):
    place = (lambda i: size - 1 - i) if reverse else (lambda i: i)
    perm = lambda pairs: [(place(i), place(j)) for i, j in pairs]
    at_first = (lambda a, b: jnp.where(low, b, a)) if reverse else (lambda a, b: jnp.where(low, a, b))
    outer = size // 2
    swap = [(i, i ^ 1) for i in range(size)]
    got = yield other, perm(swap), None
    mine = mine()
    pair = mine + got
    total = None
    if outer <= 4:
        running = pair
        for hop in range(outer - 1):
            r = yield running, perm([(2 * hop, 2 * hop + 2), (2 * hop + 1, 2 * hop + 3)]), None
            total = r if total is None else total + r
            running = r + pair
    else:
        total = yield pair, perm([(i, i + 2) for i in range(size - 2)]), None
        step = 1
        while step < outer - 1:
            r = yield total, perm([(i, i + 2 * step) for i in range(size - 2 * step)]), None
            total = total + r
            step *= 2
    return (yield at_first(total + mine, total), perm(swap), at_first(total, total + got))


def after(tied, *arrays):
    return lax.optimization_barrier((*arrays, *tied))[: len(arrays)] if tied else arrays


def drive(makers, pieces, early, finish):
    live, behind, event = [], (), 0
    waiting = list(makers)
    while waiting or live:
        if waiting:
            scan = waiting.pop(0)()
            name, (operand, pairs, answer) = len(makers) - len(waiting) - 1, next(scan)
        else:
            name, scan, result = live.pop(0)
            try:
                operand, pairs, answer = scan.send(after(behind, result)[0])
            except StopIteration as stop:
                behind = finish(name, stop.value)
                continue
        if answer is not None:
            early(name, answer)
        live.append((name, scan, lax.ppermute(operand, "seq", pairs)))
        behind = pieces.pop(event)((operand,)) if event in pieces else ()
        event += 1
    for piece in pieces.values():
        piece(())


def in_events(events):
    def in_turn(works, tied):
        for work in works:
            tied = work(tied)
        return tied

    return {event: functools.partial(in_turn, works) for event, works in sorted(events.items())}


def head_sum(a, size):
    if size & (size - 1):
        return lax.psum(a, "head")
    step = 1
    while step < size:
        a = a + lax.ppermute(a, "head", [(i, i ^ step) for i in range(size)])
        step *= 2
    return a


def body(seq_size, head_size, queries, keys, values, gain, out_grad):
    rows, width = queries.shape
    blocks, heads = rows // BLOCK, width // HEAD_DIM
    size = heads // 4
    low = lax.axis_index("seq") % 2 == 0
    gain = gain.reshape(1, width)
    unit = 2 * rows * HEAD_DIM * HEAD_DIM
    whole = ((rows, width), BF16)
    part = (rows, size * HEAD_DIM)
    state = ((size, HEAD_DIM, HEAD_DIM), F32)
    ks, vs, states, weights, atts, sums, prefixes, grads, backs = ({} for _ in range(9))

    outer = seq_size // 2
    last = 2 * (2 + (outer - 1 if outer <= 4 else (outer - 2).bit_length() + 1)) - 1


    def piece_load(groups, tied):
        got = call(
            functools.partial(load_kernel, groups, size),
            after(tied, keys, values),
            [(part, BF16)] * (2 * len(groups)) + [state] * len(groups),
            in_specs=[HBM, HBM],
            scratch=[pltpu.SemaphoreType.DMA((len(groups), 2))],
            flops=unit * size * len(groups),
            vmem=52 if len(groups) == 1 else 50,
        )
        count = len(groups)
        for n, g in enumerate(groups):
            ks[g], vs[g], states[g] = got[n], got[count + n], got[2 * count + n]
        return tuple(states[g] for g in groups)

    def piece_local(g, tied):
        (q,) = after(tied, queries)
        weights[g], atts[g] = call(
            functools.partial(local_kernel, g, size, blocks),
            [q, ks[g], vs[g]],
            [(part, BF16), (part, F32)],
            scratch=[pltpu.VMEM(part, BF16)],
            flops=4 * unit * size,
        )
        return weights[g], atts[g]

    def piece_stats(g, tied):
        (q,) = after(tied, queries)
        atts[g], sums[g] = call(
            functools.partial(stats_kernel, g, size, blocks),
            [atts[g], q, prefixes[g], out_grad, gain],
            [(part, F32), ((2, rows), F32)],
            flops=unit * size,
        )
        return atts[g], sums[g]

    def end_stats(i, answer):
        prefixes[2 * i] = answer
        return piece_stats(2 * i, ())

    piece_load([0], (low,))
    drive(
        [lambda i=i: scan_stages(states[2 * i], lambda: states[2 * i + 1], seq_size, low, False) for i in range(2)],
        in_events({
            0: [functools.partial(piece_load, [1, 2, 3])],
            3: [functools.partial(piece_local, 0), functools.partial(piece_local, 1)],
            5: [functools.partial(piece_local, 2), functools.partial(piece_local, 3)],
            last: [functools.partial(piece_stats, 1), functools.partial(piece_stats, 3)],
        }),
        lambda i, answer: prefixes.update({2 * i + 1: answer}),
        end_stats,
    )
    total = head_sum(sum(sums[g] for g in range(1, 4)) + sums[0], head_size)

    factors, inner, made, fresh, suffixes, results = [], {}, [], [], {}, []

    def piece_grad(g, tied):
        (q,) = after(tied, queries)
        grads[g], backs[g], *new = call(
            functools.partial(grad_kernel, g, size, blocks),
            [atts[g], q, out_grad, gain, *(factors or [total])],
            [(part, BF16), state] + ([] if factors else [((rows, BLOCK), F32)] * 2),
            flops=unit * size,
        )
        factors.extend(new)
        return (backs[g],)

    def piece_back(g, first, count, out, tied):
        (q,) = after(tied, queries)
        old = list(fresh) if out else []
        ins = [q, ks[g], vs[g], weights[g], grads[g], prefixes[g], atts[g], gain, factors[0]]
        ins += [a for _, *pair in old for a in pair]
        own = (rows, count * HEAD_DIM)
        specs, outs, aliases = [VMEM] * len(ins), [(own, BF16)] * 2 + [(own, F32)] * 2, {}
        out_specs, scratch = [VMEM] * 4, [pltpu.VMEM(own, BF16)] * 3
        if old:
            aliases = {len(ins) + n: 4 + n for n in range(len(made))}
            ins, specs = ins + made, specs + [HBM] * len(made)
            outs, out_specs = outs + [whole] * 2, out_specs + [HBM] * 2
            scratch.append(pltpu.SemaphoreType.DMA((len(old), 2)))
        m, q, *others = call(
            functools.partial(back_kernel, (g, first, count), [where for where, _, _ in old], size, blocks),
            ins,
            outs,
            in_specs=specs,
            out_specs=out_specs,
            scratch=scratch,
            aliases=aliases,
            flops=9 * unit * count,
        )
        inner[g, first] = (count, *others[:2])
        if old:
            made[:] = others[2:]
            fresh.clear()
        fresh.append(((g, first, count), m, q))
        return tuple(others[:2])

    def piece_flush(tied):
        ((where, m, q),) = fresh
        ins, into = [*after(tied, m), q], list(made)
        made[:] = call(
            functools.partial(flush_kernel, where, size),
            ins + into,
            [whole] * 2,
            in_specs=[VMEM] * 2 + [HBM] * len(into),
            out_specs=[HBM] * 2,
            scratch=[pltpu.SemaphoreType.DMA((2,))],
            aliases={2 + n: n for n in range(len(into))},
        )
        return tuple(made)

    def piece_last(g, tied):
        mine = [inner[key] for key in sorted(inner) if key[0] == g]
        ins = [*after(tied, ks[g]), vs[g], suffixes[g]] + [kl for _, kl, _ in mine] + [vl for _, _, vl in mine]
        results[:] = call(
            functools.partial(last_kernel, g, [count for count, _, _ in mine], size),
            ins + results,
            [whole] * 2,
            in_specs=[VMEM] * len(ins) + [HBM] * len(results),
            out_specs=[HBM] * 2,
            scratch=[pltpu.VMEM(part, BF16)] * 2 + [pltpu.SemaphoreType.DMA((2, size))],
            aliases={len(ins) + n: n for n in range(len(results))},
            flops=2 * unit * size,
        )
        return tuple(results)

    def end_last(i, answer):
        suffixes[2 * i] = answer
        return piece_last(2 * i, ())

    piece_grad(0, ())
    drive(
        [lambda i=i: scan_stages(backs[2 * i], lambda: backs[2 * i + 1], seq_size, low, True) for i in range(2)],
        in_events({
            0: [functools.partial(piece_grad, 2)],
            1: [functools.partial(piece_grad, 1), functools.partial(piece_grad, 3)],
            3: [functools.partial(piece_back, 0, 0, size, False), functools.partial(piece_back, 1, 0, size, False)],
            5: [functools.partial(piece_back, 2, 0, size, True), functools.partial(piece_back, 3, 0, size, True), piece_flush],
            last: [functools.partial(piece_last, 1), functools.partial(piece_last, 3)],
        }),
        lambda i, answer: suffixes.update({2 * i + 1: answer}),
        end_last,
    )
    return (*made, *results)


def solution(mesh):
    placed = (P("seq", "head"), P("seq", "head"), P("seq", "head"), P("head"), P("seq", "head"))
    return jax.shard_map(
        functools.partial(body, mesh.shape["seq"], mesh.shape["head"]),
        mesh=mesh,
        in_specs=placed,
        out_specs=(P("seq", "head"),) * 4,
        check_vma=False,
    )
```
